32 devices in a mesh: clip: 8 (over y, x, core), shard: 4 (over z).
Axes of the slice: x: 2, y: 2, z: 4, core: 2. Of those that a mesh axis runs over, the one named last changes fastest.
Arguments:
- tokens: bfloat16 [8, 9216, 768], P('clip', 'shard'), may hold values from -6 to 6
- scales: float32 [8, 6, 9216], P('clip', None, 'shard'), may hold values from 0.1875 to 5
- slot_params: bfloat16 [768, 128], replicated, may hold values from -2 to 2
- expand_weight: bfloat16 [64, 768, 3072], P(('clip', 'shard')), may hold values from -0.21875 to 0.21875
- expand_bias: bfloat16 [64, 3072], P(('clip', 'shard')), may hold values from -4 to 4
- reduce_weight: bfloat16 [64, 3072, 768], P(('clip', 'shard')), may hold values from -0.109375 to 0.109375
- reduce_bias: bfloat16 [64, 768], P(('clip', 'shard')), may hold values from -4 to 4
Outputs:
- mixed: bfloat16 [8, 9216, 768], P('clip', 'shard')
The draws below stay inside these ranges and needn't reach their ends.
All inputs are finite; a program needn't handle non-finite values.
Results may differ from the reference program's by a relative error of at most 0.012.
The reference program's roundings to bfloat16 on the way (of `features`, `dispatch`, `slot_inputs`, `normalized`, `hidden`, `slot_outputs` and `combine`) count: a program that leaves them out, or rounds other values in their place, can miss the bound.
Values may be sent and summed in bfloat16 or wider, within the bound.
A program may use at most 128 MiB of HBM per device.

```python
import math
import jax
import jax.numpy as jnp
from jax import lax

D = 768
FF = 3072
SLOTS = 2
BLOCK = 128
EXPERTS = 64
SLOTS_ALL = 128
CLIPS = 8
LENGTH = 9216
BLOCKS = 6


def draw_tokens(key, part):
    array_shape = (CLIPS, LENGTH, D)
    values = jax.random.truncated_normal(jax.random.fold_in(key, 1), -6.0, 6.0, array_shape, jnp.float32)
    return values.astype(jnp.bfloat16)


def draw_scales(key, part):
    array_shape = (CLIPS, BLOCKS, LENGTH)
    spread = jax.random.uniform(jax.random.fold_in(key, 3), array_shape, jnp.float32, math.log(0.25), math.log(4.0))
    ramp = 0.75 + 0.5 * jnp.arange(LENGTH, dtype=jnp.float32) / LENGTH
    values = jnp.exp(spread) * ramp
    return values


def draw_slot_params(key, part):
    array_shape = (D, SLOTS_ALL)
    values = jax.random.truncated_normal(jax.random.fold_in(key, 4), -6.0, 6.0, array_shape, jnp.float32) * (0.9 / math.sqrt(D))
    return values.astype(jnp.bfloat16)


def level_of(key, extent, shards, smallest, top_value):
    gain = 1.0
    for position, parts in shards:
        steps = jax.random.uniform(jax.random.fold_in(jax.random.fold_in(key, 6), position), (parts,), jnp.float32, smallest / len(shards), top_value / len(shards))
        gain = gain * jnp.repeat(jnp.exp(steps), extent[position] // parts).reshape((-1,) + (1,) * (len(extent) - 1 - position))
    return gain


def scatter_about(own_key, dims, width, reach, shards=(), kind=jnp.bfloat16):
    values = width * jax.random.normal(own_key, dims, jnp.float32)
    if shards:
        values = values * level_of(own_key, dims, shards, -0.22, 0.18)
    return jnp.clip(values, -reach, reach).astype(kind)


def setup_inputs(seed: int = 0) -> dict:
    streams_of = jax.random.split(jax.random.key(seed), 8)
    return {
        "tokens": draw_tokens(jax.random.fold_in(streams_of[7], 71), 0),
        "scales": draw_scales(jax.random.fold_in(streams_of[7], 71), 0),
        "slot_params": draw_slot_params(jax.random.fold_in(streams_of[7], 71), 0),
        "expand_weight": scatter_about(streams_of[3], (EXPERTS, D, FF), D ** -0.5, 0.21875, ((0, 32),)),
        "expand_bias": scatter_about(streams_of[4], (EXPERTS, FF), 1.0, 4.0, ((0, 32),)),
        "reduce_weight": scatter_about(streams_of[5], (EXPERTS, FF, D), FF ** -0.5, 0.109375, ((0, 32),)),
        "reduce_bias": scatter_about(streams_of[6], (EXPERTS, D), 1.0, 4.0, ((0, 32),)),
    }


def dequantize(quantized, block_scale):
    blocks = quantized.reshape(LENGTH, BLOCKS, BLOCK).astype(jnp.float32) * block_scale.T[:, :, None]
    return blocks.reshape(LENGTH, D).astype(jnp.bfloat16)

def clip_logits(quantized, block_scale, slot_params):
    features = dequantize(quantized, block_scale)
    return (features, jnp.dot(features, slot_params, preferred_element_type=jnp.float32))

def reference(tokens, scales, slot_params, expand_weight, expand_bias, reduce_weight, reduce_bias):

    def slot_sums(operands):
        features, logits = clip_logits(operands[0], operands[1], slot_params)
        column_peak = lax.optimization_barrier(jnp.max(logits, axis=0, keepdims=True))
        weights = jnp.exp(logits - column_peak)
        dispatch = (weights / lax.optimization_barrier(jnp.sum(weights, axis=0, keepdims=True))).astype(jnp.bfloat16)
        return jnp.dot(dispatch.T, features, preferred_element_type=jnp.float32).astype(jnp.bfloat16)
    slot_inputs = lax.map(slot_sums, (tokens, scales))
    grouped = slot_inputs.reshape(CLIPS, EXPERTS, SLOTS, D).transpose(1, 0, 2, 3).reshape(EXPERTS, CLIPS * SLOTS, D)

    def expert_apply(operands):
        slot_rows, weight_in, bias_in, weight_out, bias_out = operands
        widened = slot_rows.astype(jnp.float32)
        normalized = (widened * lax.rsqrt(lax.optimization_barrier(jnp.mean(widened * widened, axis=-1, keepdims=True)) + 1e-06)).astype(jnp.bfloat16)
        hidden = jnp.dot(normalized, weight_in, preferred_element_type=jnp.float32) + bias_in.astype(jnp.float32)
        hidden = jax.nn.gelu(hidden, approximate=False).astype(jnp.bfloat16)
        output = jnp.dot(hidden, weight_out, preferred_element_type=jnp.float32) + bias_out.astype(jnp.float32)
        return output.astype(jnp.bfloat16)
    slot_outputs = lax.map(expert_apply, (grouped, expand_weight, expand_bias, reduce_weight, reduce_bias))
    per_clip = slot_outputs.reshape(EXPERTS, CLIPS, SLOTS, D).transpose(1, 0, 2, 3).reshape(CLIPS, SLOTS_ALL, D)

    def combine_clip(operands):
        features, logits = clip_logits(operands[0], operands[1], slot_params)
        row_peak = lax.optimization_barrier(jnp.max(logits, axis=1, keepdims=True))
        weights = jnp.exp(logits - row_peak)
        combine = (weights / lax.optimization_barrier(jnp.sum(weights, axis=1, keepdims=True))).astype(jnp.bfloat16)
        return jnp.dot(combine, operands[2], preferred_element_type=jnp.float32).astype(jnp.bfloat16)
    return lax.map(combine_clip, (tokens, scales, per_clip))
```

```python
import functools
import math

import jax
import jax.numpy as jnp
from jax import lax
from jax.experimental import pallas as pl
from jax.experimental.pallas import tpu as pltpu
from jax.sharding import PartitionSpec as P

F32 = jnp.float32
BF16 = jnp.bfloat16
MESH = pl.DeviceIdType.MESH
CHUNK = 256
HIDDEN_CHUNK = 768


def dot(a, b, contract=((1,), (0,))):
    return lax.dot_general(a, b, (contract, ((), ())), preferred_element_type=F32)


def iota(shape, axis):
    return lax.broadcasted_iota(jnp.int32, shape, axis)


def top_half(shape, rows):
    return iota(shape, 0) % (2 * rows) < rows


def spread(value, rows):
    count, dim = value.shape
    left, right = value[:, : dim // 2], value[:, dim // 2 :]
    top = top_half(left.shape, rows)
    even = jnp.where(top, left, pltpu.roll(right, rows, 0))
    odd = jnp.where(top, pltpu.roll(left, count - rows, 0), right)
    shape = (count // (2 * rows), 2 * rows, dim // 2)
    return even.reshape(shape), odd.reshape(shape)


def unspread(even, odd, rows):
    shape = (even.shape[0] * 2 * rows, even.shape[2])
    even, odd = even.reshape(shape), odd.reshape(shape)
    top = top_half(shape, rows)
    left = jnp.where(top, even, pltpu.roll(odd, rows, 0))
    right = jnp.where(top, pltpu.roll(even, shape[0] - rows, 0), odd)
    return jnp.concatenate([left, right], axis=1)


def kernel(
    clips,
    shards,
    tokens,
    scales,
    slot_params,
    w1,
    b1,
    w2,
    b2,
    combine,
    returned,
    feat,
    scale_v,
    params_v,
    w1_v,
    b1_v,
    w2_v,
    b2_v,
    logits,
    lifted,
    stats_out,
    stats,
    lift_out,
    lift,
    partial_out,
    sums,
    back_out,
    back_in,
    local_sem,
    token_sem,
    send_a,
    recv_a,
    send_b,
    recv_b,
    send_c,
    recv_c,
    send_d,
    recv_d,
):
    c_me, s_me = lax.axis_index("clip"), lax.axis_index("shard")
    count, dim = feat.shape
    blocks = scale_v.shape[0]
    width = dim // blocks
    slots = params_v.shape[1]
    experts, _, ff = w1_v.shape
    rows = slots // (clips * shards)
    each = rows // experts
    group = clips * rows
    devices = clips * shards
    me = c_me * shards + s_me
    chunks = count // CHUNK

    def span(i):
        return pl.ds(i * CHUNK, CHUNK)

    load_scale = pltpu.make_async_copy(scales, scale_v, local_sem.at[0])
    load_params = pltpu.make_async_copy(slot_params, params_v, local_sem.at[1])
    load_params.start()
    load_scale.start()
    for i in range(chunks):
        pltpu.make_async_copy(
            tokens.at[pl.ds(i * CHUNK, CHUNK)], feat.at[pl.ds(i * CHUNK, CHUNK)], token_sem.at[i]
        ).start()
    weight_loads = [
        pltpu.make_async_copy(w1, w1_v, local_sem.at[2]),
        pltpu.make_async_copy(b1, b1_v, local_sem.at[3]),
        pltpu.make_async_copy(w2, w2_v, local_sem.at[4]),
        pltpu.make_async_copy(b2, b2_v, local_sem.at[5]),
    ]
    barrier = pltpu.get_barrier_semaphore()

    def place(d):
        at = lax.rem(me + d, devices)
        return at, at // shards, lax.rem(at, shards)

    def greet(d, carry):
        _, c, s = place(d)
        pl.semaphore_signal(barrier, inc=1, device_id=(c, s), device_id_type=MESH)
        return carry

    lax.fori_loop(1, devices, greet, 0)
    load_params.wait()
    load_scale.wait()

    peak = jnp.full((1, slots), -jnp.inf, F32)
    for i in range(chunks):
        at = span(i)
        pltpu.make_async_copy(tokens.at[at], feat.at[at], token_sem.at[i]).wait()
        if i == chunks - 1:
            for load in weight_loads:
                load.start()
        scale = scale_v[:, 0, at].T
        scaled = jnp.concatenate(
            [
                feat[at, b * width : (b + 1) * width].astype(F32) * scale[:, b : b + 1]
                for b in range(blocks)
            ],
            axis=1,
        ).astype(BF16)
        feat[at, :] = scaled
        value = dot(scaled, params_v[...])
        logits[at, :] = value
        peak = jnp.maximum(peak, jnp.max(value, axis=0, keepdims=True))

    total = jnp.zeros((1, slots), F32)
    for i in range(chunks):
        at = span(i)
        value = jnp.exp(logits[at, :] - peak)
        total = total + jnp.sum(value, axis=0, keepdims=True)
        high = value.astype(BF16)
        low = (value - high.astype(F32)).astype(BF16)
        lifted[at, :slots] = high
        lifted[at, slots:] = low
    stats_out[0:1, :] = peak
    stats_out[1:2, :] = total
    stats[s_me] = stats_out[...]
    pl.semaphore_wait(barrier, devices - 1)

    def send_stats(d):
        return pltpu.make_async_remote_copy(
            src_ref=stats_out,
            dst_ref=stats.at[s_me],
            send_sem=send_a.at[d],
            recv_sem=recv_a.at[s_me],
            device_id=(c_me, lax.rem(s_me + d, shards)),
            device_id_type=MESH,
        )

    for d in range(1, shards):
        send_stats(d).start()
    partial = dot(lifted[...], feat[...], ((0,), (0,)))
    partial = partial[:slots] + partial[slots:]
    even, odd = spread(partial, rows)
    partial_out[:, 0] = even.astype(BF16)
    partial_out[:, 1] = odd.astype(BF16)

    def aim(d):
        c = lax.rem(c_me + lax.rem(d, clips), clips)
        s = lax.rem(s_me + d // clips, shards)
        return c * shards + s, c, s

    def send_sum(d):
        to, c, s = aim(d)
        return pltpu.make_async_remote_copy(
            src_ref=partial_out.at[to // 2, lax.rem(to, 2)],
            dst_ref=sums.at[s_me, c_me // 2, lax.rem(c_me, 2)],
            send_sem=send_b.at[d],
            recv_sem=recv_b.at[me],
            device_id=(c, s),
            device_id_type=MESH,
        )

    def start_sum(d, carry):
        send_sum(devices - d).start()
        return carry

    lax.fori_loop(1, devices, start_sum, 0)
    sums[s_me, c_me // 2, lax.rem(c_me, 2)] = partial_out[me // 2, lax.rem(me, 2)]

    for d in range(1, shards):
        origin = stats.at[lax.rem(s_me + d, shards)]
        pltpu.make_async_copy(origin, origin, recv_a.at[lax.rem(s_me + d, shards)]).wait()
    peaks = [stats[s, 0:1] for s in range(shards)]
    top = functools.reduce(jnp.maximum, peaks)
    lifts = [jnp.exp(p - top) for p in peaks]
    total = sum(stats[s, 1:2] * lifts[s] for s in range(shards))
    for s in range(shards):
        lift_out[s : s + 1] = lifts[s] / total
    lift[c_me] = lift_out[...]

    def send_lift(d):
        return pltpu.make_async_remote_copy(
            src_ref=lift_out,
            dst_ref=lift.at[c_me],
            send_sem=send_d.at[d],
            recv_sem=recv_d.at[c_me],
            device_id=(lax.rem(c_me + d, clips), s_me),
            device_id_type=MESH,
        )

    for d in range(1, clips):
        send_lift(d).start()

    for i in range(chunks):
        at = span(i)
        value = logits[at, :]
        weights = jnp.exp(value - jnp.max(value, axis=1, keepdims=True))
        combine[at, :] = (weights / jnp.sum(weights, axis=1, keepdims=True)).astype(BF16)

    def await_sum(d, carry):
        origin, c, s = place(d)
        landed = sums.at[s, c // 2, lax.rem(c, 2)]
        pltpu.make_async_copy(landed, landed, recv_b.at[origin]).wait()
        return carry

    for d in range(1, clips):
        c = lax.rem(c_me + d, clips)
        pltpu.make_async_copy(lift.at[c], lift.at[c], recv_d.at[c]).wait()

    lax.fori_loop(1, devices, await_sum, 0)
    lane = iota((2 * rows, slots), 1) == me * rows + iota((2 * rows, slots), 0) % rows
    weighted = []
    for c in range(clips):
        value = jnp.zeros(sums.shape[3:], F32)
        for s in range(shards):
            own = jnp.sum(jnp.where(lane, lift[c, s : s + 1], 0.0), axis=1, keepdims=True)
            value = value + sums[s, c // 2, c % 2].astype(F32) * own
        weighted.append(value[None])
    even, odd = (jnp.concatenate(weighted[p::2], axis=0) for p in range(2))
    wide = unspread(even, odd, rows).astype(BF16).astype(F32)

    mean = jnp.mean(wide * wide, axis=-1, keepdims=True)
    normalized = (wide * lax.rsqrt(mean + 1e-06)).astype(BF16)
    for load in weight_loads:
        load.wait()

    def mine(shape, expert):
        return (iota(shape, 0) % rows) // each == expert

    def choose(values):
        chosen = values[0]
        for e in range(1, experts):
            chosen = jnp.where(mine(chosen.shape, e), values[e], chosen)
        return chosen

    def spread_bias(ref, at):
        value = ref[:, at].astype(F32)
        size = (group, value.shape[1])
        return choose([jnp.broadcast_to(value[e : e + 1], size) for e in range(experts)])

    def expert_step(f, outs):
        at = pl.ds(pl.multiple_of(f * HIDDEN_CHUNK, HIDDEN_CHUNK), HIDDEN_CHUNK)
        before = choose([dot(normalized, w1_v[e, :, at]) for e in range(experts)])
        before = before + spread_bias(b1_v, at)
        hidden = (0.5 * before * (1.0 + lax.erf(before * math.sqrt(0.5)))).astype(BF16)
        return tuple(outs[e] + dot(hidden, w2_v[e, at, :]) for e in range(experts))

    outs = tuple(jnp.zeros((group, dim), F32) for _ in range(experts))
    outs = lax.fori_loop(0, ff // HIDDEN_CHUNK, expert_step, outs, unroll=True)
    result = (choose(outs) + spread_bias(b2_v, slice(None))).astype(BF16).astype(F32)
    even, odd = spread(result, rows)
    back_out[:, 0] = even.astype(BF16)
    back_out[:, 1] = odd.astype(BF16)

    def send_back(d):
        to, c, s = place(d)
        return pltpu.make_async_remote_copy(
            src_ref=back_out.at[c // 2, lax.rem(c, 2)],
            dst_ref=back_in.at[me // 2, lax.rem(me, 2)],
            send_sem=send_c.at[d],
            recv_sem=recv_c.at[me],
            device_id=(c, s),
            device_id_type=MESH,
        )

    def start_back(d, carry):
        send_back(d).start()
        return carry

    lax.fori_loop(1, devices, start_back, 0)
    back_in[me // 2, lax.rem(me, 2)] = back_out[c_me // 2, lax.rem(c_me, 2)]

    def await_back(d, carry):
        origin, c, s = place(d)
        landed = back_in.at[origin // 2, lax.rem(origin, 2)]
        pltpu.make_async_copy(landed, landed, recv_c.at[origin]).wait()
        return carry

    lax.fori_loop(1, devices, await_back, 0)
    value = back_in[...].astype(F32)
    returned[...] = unspread(value[:, 0], value[:, 1], rows).astype(BF16)

    for d in range(1, shards):
        send_stats(d).wait_send()
    for d in range(1, clips):
        send_lift(d).wait_send()

    def finish(d, carry):
        send_sum(d).wait_send()
        send_back(d).wait_send()
        return carry

    lax.fori_loop(1, devices, finish, 0)


def mix(combine, returned, mixed, buffer, sems):
    stores = []
    for i in range(combine.shape[0] // CHUNK):
        at = pl.ds(i * CHUNK, CHUNK)
        buffer[at, :] = dot(combine[at, :], returned[...]).astype(BF16)
        store = pltpu.make_async_copy(buffer.at[at], mixed.at[at], sems.at[i])
        store.start()
        stores.append(store)
    for store in stores:
        store.wait()


def local(clips, shards, tokens, scales, slot_params, w1, b1, w2, b2):
    count, dim = tokens.shape[1:]
    blocks = scales.shape[1]
    slots = slot_params.shape[1]
    rows = slots // (clips * shards)
    devices = clips * shards
    piece = (2, 2 * rows, dim // 2)
    combine, returned = pl.pallas_call(
        functools.partial(kernel, clips, shards),
        out_shape=(pltpu.VMEM((count, slots), BF16), pltpu.VMEM((slots, dim), BF16)),
        in_specs=[pl.BlockSpec(memory_space=pltpu.HBM)] * 7,
        out_specs=(pl.BlockSpec(memory_space=pltpu.VMEM), pl.BlockSpec(memory_space=pltpu.VMEM)),
        scratch_shapes=[
            pltpu.VMEM((count, dim), BF16),
            pltpu.VMEM((blocks, 1, count), F32),
            pltpu.VMEM(slot_params.shape, BF16),
            pltpu.VMEM(w1.shape, BF16),
            pltpu.VMEM(b1.shape, BF16),
            pltpu.VMEM(w2.shape, BF16),
            pltpu.VMEM(b2.shape, BF16),
            pltpu.VMEM((count, slots), F32),
            pltpu.VMEM((count, 2 * slots), BF16),
            pltpu.VMEM((2, slots), F32),
            pltpu.VMEM((shards, 2, slots), F32),
            pltpu.VMEM((shards, slots), F32),
            pltpu.VMEM((clips, shards, slots), F32),
            pltpu.VMEM((devices // 2,) + piece, BF16),
            pltpu.VMEM((shards, clips // 2) + piece, BF16),
            pltpu.VMEM((clips // 2,) + piece, BF16),
            pltpu.VMEM((devices // 2,) + piece, BF16),
            pltpu.SemaphoreType.DMA((7,)),
            pltpu.SemaphoreType.DMA((count // CHUNK,)),
            pltpu.SemaphoreType.DMA((devices,)),
            pltpu.SemaphoreType.DMA((devices,)),
            pltpu.SemaphoreType.DMA((devices,)),
            pltpu.SemaphoreType.DMA((devices,)),
            pltpu.SemaphoreType.DMA((devices,)),
            pltpu.SemaphoreType.DMA((devices,)),
            pltpu.SemaphoreType.DMA((clips,)),
            pltpu.SemaphoreType.DMA((clips,)),
        ],
        compiler_params=pltpu.CompilerParams(
            collective_id=0, has_side_effects=True, vmem_limit_bytes=57 << 20
        ),
        name="slots",
    )(tokens[0], scales.transpose(1, 0, 2), slot_params, w1, b1, w2, b2)
    mixed = pl.pallas_call(
        mix,
        out_shape=jax.ShapeDtypeStruct((count, dim), BF16),
        in_specs=[pl.BlockSpec(memory_space=pltpu.VMEM)] * 2,
        out_specs=pl.BlockSpec(memory_space=pl.ANY),
        scratch_shapes=[
            pltpu.VMEM((count, dim), BF16),
            pltpu.SemaphoreType.DMA((count // CHUNK,)),
        ],
        compiler_params=pltpu.CompilerParams(vmem_limit_bytes=16 << 20),
        name="mix",
    )(combine, returned)
    return mixed[None]


def solution(mesh):
    placed = (
        P("clip", "shard", None),
        P("clip", None, "shard"),
        P(),
        P(("clip", "shard"), None, None),
        P(("clip", "shard"), None),
        P(("clip", "shard"), None, None),
        P(("clip", "shard"), None),
    )
    return jax.shard_map(
        functools.partial(local, mesh.shape["clip"], mesh.shape["shard"]),
        mesh=mesh,
        in_specs=placed,
        out_specs=P("clip", "shard", None),
        check_vma=False,
    )
```

```python
import functools
import math

import jax
import jax.numpy as jnp
from jax import lax
from jax.experimental import pallas as pl
from jax.experimental.pallas import tpu as pltpu
from jax.sharding import PartitionSpec as P

F32 = jnp.float32
BF16 = jnp.bfloat16
MESH = pl.DeviceIdType.MESH
CHUNKS = 2
MIX_CHUNK = 256
HIDDEN_CHUNK = 768


def dot(a, b, contract=((1,), (0,))):
    return lax.dot_general(a, b, (contract, ((), ())), preferred_element_type=F32)


def iota(shape, axis):
    return lax.broadcasted_iota(jnp.int32, shape, axis)


def top_half(shape, rows):
    return iota(shape, 0) % (2 * rows) < rows


def spread(value, rows):
    count, dim = value.shape
    left, right = value[:, : dim // 2], value[:, dim // 2 :]
    top = top_half(left.shape, rows)
    even = jnp.where(top, left, pltpu.roll(right, rows, 0))
    odd = jnp.where(top, pltpu.roll(left, count - rows, 0), right)
    shape = (count // (2 * rows), 2 * rows, dim // 2)
    return even.reshape(shape), odd.reshape(shape)


def unspread(even, odd, rows):
    shape = (even.shape[0] * 2 * rows, even.shape[2])
    even, odd = even.reshape(shape), odd.reshape(shape)
    top = top_half(shape, rows)
    left = jnp.where(top, even, pltpu.roll(odd, rows, 0))
    right = jnp.where(top, pltpu.roll(even, shape[0] - rows, 0), odd)
    return jnp.concatenate([left, right], axis=1)


def kernel(
    clips,
    shards,
    tokens,
    scales,
    slot_params,
    w1,
    b1,
    w2,
    b2,
    combine,
    returned,
    feat,
    scale_v,
    params_v,
    w1_v,
    b1_v,
    w2_v,
    b2_v,
    logits,
    lifted,
    stats_out,
    stats,
    lift_out,
    lift,
    partial_out,
    sums,
    back_out,
    back_in,
    local_sem,
    token_sem,
    send_a,
    recv_a,
    send_b,
    recv_b,
    send_c,
    recv_c,
    send_d,
    recv_d,
):
    c_me, s_me = lax.axis_index("clip"), lax.axis_index("shard")
    count, dim = feat.shape
    blocks = scale_v.shape[0]
    width = dim // blocks
    slots = params_v.shape[1]
    experts, _, ff = w1_v.shape
    rows = slots // (clips * shards)
    each = rows // experts
    group = clips * rows
    devices = clips * shards
    me = c_me * shards + s_me
    chunk = count // CHUNKS

    def span(i):
        return pl.ds(i * chunk, chunk)

    load_scale = pltpu.make_async_copy(scales, scale_v, local_sem.at[0])
    load_params = pltpu.make_async_copy(slot_params, params_v, local_sem.at[1])
    load_params.start()
    load_scale.start()
    for i in range(CHUNKS):
        pltpu.make_async_copy(tokens.at[span(i)], feat.at[span(i)], token_sem.at[i]).start()
    weight_loads = [
        pltpu.make_async_copy(w1, w1_v, local_sem.at[2]),
        pltpu.make_async_copy(b1, b1_v, local_sem.at[3]),
        pltpu.make_async_copy(w2, w2_v, local_sem.at[4]),
        pltpu.make_async_copy(b2, b2_v, local_sem.at[5]),
    ]
    barrier = pltpu.get_barrier_semaphore()

    def place(d):
        at = lax.rem(me + d, devices)
        return at, at // shards, lax.rem(at, shards)

    def greet(d, carry):
        _, c, s = place(d)
        pl.semaphore_signal(barrier, inc=1, device_id=(c, s), device_id_type=MESH)
        return carry

    lax.fori_loop(1, devices, greet, 0)
    load_params.wait()
    load_scale.wait()

    peak = jnp.full((1, slots), -jnp.inf, F32)
    for i in range(CHUNKS):
        at = span(i)
        pltpu.make_async_copy(tokens.at[at], feat.at[at], token_sem.at[i]).wait()
        if i == CHUNKS - 1:
            for load in weight_loads:
                load.start()
        scaled = jnp.concatenate(
            [
                feat[at, b * width : (b + 1) * width].astype(F32)
                * jnp.broadcast_to(scale_v[b, 0:1, at], (width, chunk)).T
                for b in range(blocks)
            ],
            axis=1,
        ).astype(BF16)
        feat[at, :] = scaled
        value = dot(scaled, params_v[...])
        logits[at, :] = value
        peak = jnp.maximum(peak, jnp.max(value, axis=0, keepdims=True))

    total = jnp.zeros((1, slots), F32)
    for i in range(CHUNKS):
        at = span(i)
        value = jnp.exp(logits[at, :] - peak)
        total = total + jnp.sum(value, axis=0, keepdims=True)
        lifted[at, :] = value.astype(BF16)
    stats_out[0:1, :] = peak
    stats_out[1:2, :] = total
    stats[s_me] = stats_out[...]
    pl.semaphore_wait(barrier, devices - 1)

    def send_stats(d):
        return pltpu.make_async_remote_copy(
            src_ref=stats_out,
            dst_ref=stats.at[s_me],
            send_sem=send_a.at[d],
            recv_sem=recv_a.at[s_me],
            device_id=(c_me, lax.rem(s_me + d, shards)),
            device_id_type=MESH,
        )

    for d in range(1, shards):
        send_stats(d).start()
    partial = dot(lifted[...], feat[...], ((0,), (0,)))
    even, odd = spread(partial, rows)
    partial_out[:, 0] = even.astype(BF16)
    partial_out[:, 1] = odd.astype(BF16)

    def aim(k):
        c, s = lax.rem(c_me + lax.rem(k, clips), clips), k // clips
        return c * shards + s, c, s

    def send_sum(k):
        to, c, s = aim(k)
        return pltpu.make_async_remote_copy(
            src_ref=partial_out.at[to // 2, lax.rem(to, 2)],
            dst_ref=sums.at[s_me, c_me // 2, lax.rem(c_me, 2)],
            send_sem=send_b.at[to],
            recv_sem=recv_b.at[me],
            device_id=(c, s),
            device_id_type=MESH,
        )

    def start_sum(k, carry):
        @pl.when(aim(k)[0] != me)
        def _():
            send_sum(k).start()

        return carry

    lax.fori_loop(0, devices, start_sum, 0)
    sums[s_me, c_me // 2, lax.rem(c_me, 2)] = partial_out[me // 2, lax.rem(me, 2)]

    for d in range(1, shards):
        origin = stats.at[lax.rem(s_me + d, shards)]
        pltpu.make_async_copy(origin, origin, recv_a.at[lax.rem(s_me + d, shards)]).wait()
    peaks = [stats[s, 0:1] for s in range(shards)]
    top = functools.reduce(jnp.maximum, peaks)
    lifts = [jnp.exp(p - top) for p in peaks]
    total = sum(stats[s, 1:2] * lifts[s] for s in range(shards))
    for s in range(shards):
        lift_out[s : s + 1] = lifts[s] / total
    lift[c_me] = lift_out[...]

    def send_lift(d):
        return pltpu.make_async_remote_copy(
            src_ref=lift_out,
            dst_ref=lift.at[c_me],
            send_sem=send_d.at[d],
            recv_sem=recv_d.at[c_me],
            device_id=(lax.rem(c_me + d, clips), s_me),
            device_id_type=MESH,
        )

    for d in range(1, clips):
        send_lift(d).start()

    for i in range(CHUNKS):
        at = span(i)
        value = logits[at, :]
        weights = jnp.exp(value - jnp.max(value, axis=1, keepdims=True))
        combine[at, :] = (weights / jnp.sum(weights, axis=1, keepdims=True)).astype(BF16)

    def await_sum(d, carry):
        origin, c, s = place(d)
        landed = sums.at[s, c // 2, lax.rem(c, 2)]
        pltpu.make_async_copy(landed, landed, recv_b.at[origin]).wait()
        return carry

    for d in range(1, clips):
        c = lax.rem(c_me + d, clips)
        pltpu.make_async_copy(lift.at[c], lift.at[c], recv_d.at[c]).wait()

    lax.fori_loop(1, devices, await_sum, 0)
    lane = iota((2 * rows, slots), 1) == me * rows + iota((2 * rows, slots), 0) % rows
    weighted = []
    for c in range(clips):
        value = jnp.zeros(sums.shape[3:], F32)
        for s in range(shards):
            own = jnp.sum(jnp.where(lane, lift[c, s : s + 1], 0.0), axis=1, keepdims=True)
            value = value + sums[s, c // 2, c % 2].astype(F32) * own
        weighted.append(value[None])
    even, odd = (jnp.concatenate(weighted[p::2], axis=0) for p in range(2))
    wide = unspread(even, odd, rows).astype(BF16).astype(F32)

    mean = jnp.mean(wide * wide, axis=-1, keepdims=True)
    normalized = (wide * lax.rsqrt(mean + 1e-06)).astype(BF16)
    for load in weight_loads:
        load.wait()

    def mine(shape, expert):
        return (iota(shape, 0) % rows) // each == expert

    def choose(values):
        chosen = values[0]
        for e in range(1, experts):
            chosen = jnp.where(mine(chosen.shape, e), values[e], chosen)
        return chosen

    def spread_bias(ref, at):
        value = ref[:, at].astype(F32)
        size = (group, value.shape[1])
        return choose([jnp.broadcast_to(value[e : e + 1], size) for e in range(experts)])

    def expert_step(f, outs):
        at = pl.ds(pl.multiple_of(f * HIDDEN_CHUNK, HIDDEN_CHUNK), HIDDEN_CHUNK)
        before = choose([dot(normalized, w1_v[e, :, at]) for e in range(experts)])
        before = before + spread_bias(b1_v, at)
        hidden = (0.5 * before * (1.0 + lax.erf(before * math.sqrt(0.5)))).astype(BF16)
        return tuple(outs[e] + dot(hidden, w2_v[e, at, :]) for e in range(experts))

    outs = tuple(jnp.zeros((group, dim), F32) for _ in range(experts))
    outs = lax.fori_loop(0, ff // HIDDEN_CHUNK, expert_step, outs, unroll=True)
    result = (choose(outs) + spread_bias(b2_v, slice(None))).astype(BF16).astype(F32)
    even, odd = spread(result, rows)
    back_out[:, 0] = even.astype(BF16)
    back_out[:, 1] = odd.astype(BF16)

    def aim_back(k):
        c, s = lax.rem(k, clips), k // clips
        return c * shards + s, c, s

    def send_back(k):
        to, c, s = aim_back(k)
        return pltpu.make_async_remote_copy(
            src_ref=back_out.at[c // 2, lax.rem(c, 2)],
            dst_ref=back_in.at[me // 2, lax.rem(me, 2)],
            send_sem=send_c.at[to],
            recv_sem=recv_c.at[me],
            device_id=(c, s),
            device_id_type=MESH,
        )

    def start_back(k, carry):
        @pl.when(aim_back(k)[0] != me)
        def _():
            send_back(k).start()

        return carry

    lax.fori_loop(0, devices, start_back, 0)
    back_in[me // 2, lax.rem(me, 2)] = back_out[c_me // 2, lax.rem(c_me, 2)]

    def await_back(d, carry):
        origin, c, s = place(d)
        landed = back_in.at[origin // 2, lax.rem(origin, 2)]
        pltpu.make_async_copy(landed, landed, recv_c.at[origin]).wait()
        return carry

    lax.fori_loop(1, devices, await_back, 0)
    value = back_in[...].astype(F32)
    returned[...] = unspread(value[:, 0], value[:, 1], rows).astype(BF16)

    for d in range(1, shards):
        send_stats(d).wait_send()
    for d in range(1, clips):
        send_lift(d).wait_send()

    def finish(k, carry):
        @pl.when(aim(k)[0] != me)
        def _():
            send_sum(k).wait_send()

        @pl.when(aim_back(k)[0] != me)
        def _():
            send_back(k).wait_send()

        return carry

    lax.fori_loop(0, devices, finish, 0)


def mix(combine, returned, mixed, buffer, sems):
    stores = []
    for i in range(combine.shape[0] // MIX_CHUNK):
        at = pl.ds(i * MIX_CHUNK, MIX_CHUNK)
        buffer[at, :] = dot(combine[at, :], returned[...]).astype(BF16)
        store = pltpu.make_async_copy(buffer.at[at], mixed.at[at], sems.at[i])
        store.start()
        stores.append(store)
    for store in stores:
        store.wait()


def local(clips, shards, tokens, scales, slot_params, w1, b1, w2, b2):
    count, dim = tokens.shape[1:]
    blocks = scales.shape[1]
    slots = slot_params.shape[1]
    rows = slots // (clips * shards)
    devices = clips * shards
    piece = (2, 2 * rows, dim // 2)
    combine, returned = pl.pallas_call(
        functools.partial(kernel, clips, shards),
        out_shape=(pltpu.VMEM((count, slots), BF16), pltpu.VMEM((slots, dim), BF16)),
        in_specs=[pl.BlockSpec(memory_space=pltpu.HBM)] * 7,
        out_specs=(pl.BlockSpec(memory_space=pltpu.VMEM), pl.BlockSpec(memory_space=pltpu.VMEM)),
        scratch_shapes=[
            pltpu.VMEM((count, dim), BF16),
            pltpu.VMEM((blocks, 1, count), F32),
            pltpu.VMEM(slot_params.shape, BF16),
            pltpu.VMEM(w1.shape, BF16),
            pltpu.VMEM(b1.shape, BF16),
            pltpu.VMEM(w2.shape, BF16),
            pltpu.VMEM(b2.shape, BF16),
            pltpu.VMEM((count, slots), F32),
            pltpu.VMEM((count, slots), BF16),
            pltpu.VMEM((2, slots), F32),
            pltpu.VMEM((shards, 2, slots), F32),
            pltpu.VMEM((shards, slots), F32),
            pltpu.VMEM((clips, shards, slots), F32),
            pltpu.VMEM((devices // 2,) + piece, BF16),
            pltpu.VMEM((shards, clips // 2) + piece, BF16),
            pltpu.VMEM((clips // 2,) + piece, BF16),
            pltpu.VMEM((devices // 2,) + piece, BF16),
            pltpu.SemaphoreType.DMA((7,)),
            pltpu.SemaphoreType.DMA((CHUNKS,)),
            pltpu.SemaphoreType.DMA((devices,)),
            pltpu.SemaphoreType.DMA((devices,)),
            pltpu.SemaphoreType.DMA((devices,)),
            pltpu.SemaphoreType.DMA((devices,)),
            pltpu.SemaphoreType.DMA((devices,)),
            pltpu.SemaphoreType.DMA((devices,)),
            pltpu.SemaphoreType.DMA((clips,)),
            pltpu.SemaphoreType.DMA((clips,)),
        ],
        compiler_params=pltpu.CompilerParams(
            collective_id=0, has_side_effects=True, vmem_limit_bytes=57 << 20
        ),
        name="slots",
    )(tokens[0], scales.transpose(1, 0, 2), slot_params, w1, b1, w2, b2)
    mixed = pl.pallas_call(
        mix,
        out_shape=jax.ShapeDtypeStruct((count, dim), BF16),
        in_specs=[pl.BlockSpec(memory_space=pltpu.VMEM)] * 2,
        out_specs=pl.BlockSpec(memory_space=pl.ANY),
        scratch_shapes=[
            pltpu.VMEM((count, dim), BF16),
            pltpu.SemaphoreType.DMA((count // MIX_CHUNK,)),
        ],
        compiler_params=pltpu.CompilerParams(vmem_limit_bytes=16 << 20),
        name="mix",
    )(combine, returned)
    return mixed[None]


def solution(mesh):
    placed = (
        P("clip", "shard", None),
        P("clip", None, "shard"),
        P(),
        P(("clip", "shard"), None, None),
        P(("clip", "shard"), None),
        P(("clip", "shard"), None, None),
        P(("clip", "shard"), None),
    )
    return jax.shard_map(
        functools.partial(local, mesh.shape["clip"], mesh.shape["shard"]),
        mesh=mesh,
        in_specs=placed,
        out_specs=P("clip", "shard", None),
        check_vma=False,
    )
```

```python
import functools
import math

import jax
import jax.numpy as jnp
from jax import lax
from jax.experimental import pallas as pl
from jax.experimental.pallas import tpu as pltpu
from jax.sharding import PartitionSpec as P

F32 = jnp.float32
BF16 = jnp.bfloat16
MESH = pl.DeviceIdType.MESH
CHUNKS = 2
MIX_CHUNK = 256
HIDDEN_CHUNK = 768


def dot(a, b, contract=((1,), (0,))):
    return lax.dot_general(a, b, (contract, ((), ())), preferred_element_type=F32)


def iota(shape, axis):
    return lax.broadcasted_iota(jnp.int32, shape, axis)


def top_half(shape, rows):
    return iota(shape, 0) % (2 * rows) < rows


def spread(value, rows):
    count, dim = value.shape
    left, right = value[:, : dim // 2], value[:, dim // 2 :]
    top = top_half(left.shape, rows)
    even = jnp.where(top, left, pltpu.roll(right, rows, 0))
    odd = jnp.where(top, pltpu.roll(left, count - rows, 0), right)
    shape = (count // (2 * rows), 2 * rows, dim // 2)
    return even.reshape(shape), odd.reshape(shape)


def unspread(even, odd, rows):
    shape = (even.shape[0] * 2 * rows, even.shape[2])
    even, odd = even.reshape(shape), odd.reshape(shape)
    top = top_half(shape, rows)
    left = jnp.where(top, even, pltpu.roll(odd, rows, 0))
    right = jnp.where(top, pltpu.roll(even, shape[0] - rows, 0), odd)
    return jnp.concatenate([left, right], axis=1)


def kernel(
    clips,
    shards,
    tokens,
    scales,
    slot_params,
    w1,
    b1,
    w2,
    b2,
    combine,
    returned,
    feat,
    scale_v,
    params_v,
    w1_v,
    b1_v,
    w2_v,
    b2_v,
    logits,
    lifted,
    stats_out,
    stats,
    lift_out,
    lift,
    partial_out,
    sums,
    back_out,
    back_in,
    local_sem,
    token_sem,
    sem,
):
    c_me, s_me = lax.axis_index("clip"), lax.axis_index("shard")
    count, dim = feat.shape
    blocks = scale_v.shape[0]
    width = dim // blocks
    slots = params_v.shape[1]
    experts, _, ff = w1_v.shape
    rows = slots // (clips * shards)
    each = rows // experts
    group = clips * rows
    devices = clips * shards
    me = c_me * shards + s_me
    chunk = count // CHUNKS

    def span(i):
        return pl.ds(i * chunk, chunk)

    load_scale = pltpu.make_async_copy(scales, scale_v, local_sem.at[0])
    load_params = pltpu.make_async_copy(slot_params, params_v, local_sem.at[1])
    load_params.start()
    load_scale.start()
    for i in range(CHUNKS):
        pltpu.make_async_copy(tokens.at[span(i)], feat.at[span(i)], token_sem.at[i]).start()
    weight_loads = [
        pltpu.make_async_copy(w1, w1_v, local_sem.at[2]),
        pltpu.make_async_copy(b1, b1_v, local_sem.at[3]),
        pltpu.make_async_copy(w2, w2_v, local_sem.at[4]),
        pltpu.make_async_copy(b2, b2_v, local_sem.at[5]),
    ]
    barrier = pltpu.get_barrier_semaphore()

    def place(d):
        at = lax.rem(me + d, devices)
        return at, at // shards, lax.rem(at, shards)

    def greet(d, carry):
        _, c, s = place(d)
        pl.semaphore_signal(barrier, inc=1, device_id=(c, s), device_id_type=MESH)
        return carry

    lax.fori_loop(1, devices, greet, 0)
    load_params.wait()
    load_scale.wait()

    peak = jnp.full((1, slots), -jnp.inf, F32)
    for i in range(CHUNKS):
        at = span(i)
        pltpu.make_async_copy(tokens.at[at], feat.at[at], token_sem.at[i]).wait()
        if i == CHUNKS - 1:
            for load in weight_loads:
                load.start()
        scaled = jnp.concatenate(
            [
                feat[at, b * width : (b + 1) * width].astype(F32)
                * jnp.broadcast_to(scale_v[b, 0:1, at], (width, chunk)).T
                for b in range(blocks)
            ],
            axis=1,
        ).astype(BF16)
        feat[at, :] = scaled
        value = dot(scaled, params_v[...])
        logits[at, :] = value
        peak = jnp.maximum(peak, jnp.max(value, axis=0, keepdims=True))

    total = jnp.zeros((1, slots), F32)
    for i in range(CHUNKS):
        at = span(i)
        value = jnp.exp(logits[at, :] - peak)
        total = total + jnp.sum(value, axis=0, keepdims=True)
        lifted[at, :] = value.astype(BF16)
    stats_out[0:1, :] = peak
    stats_out[1:2, :] = total
    stats[s_me] = stats_out[...]
    pl.semaphore_wait(barrier, devices - 1)

    def send_stats(d):
        return pltpu.make_async_remote_copy(
            src_ref=stats_out,
            dst_ref=stats.at[s_me],
            send_sem=sem.at[0],
            recv_sem=sem.at[1],
            device_id=(c_me, lax.rem(s_me + d, shards)),
            device_id_type=MESH,
        )

    for d in range(1, shards):
        send_stats(d).start()
    partial = dot(lifted[...], feat[...], ((0,), (0,)))
    even, odd = spread(partial, rows)
    pairs = (devices // 2, 2, 2 * rows, dim // 2)
    both = jnp.concatenate([even[:, None], odd[:, None]], axis=1).astype(BF16)
    partial_out[...] = both.reshape(partial_out.shape)

    def aim(k):
        c, s = lax.rem(c_me + lax.rem(k, clips), clips), k // clips
        return c * shards + s, c, s

    def send_sum(k):
        to, c, s = aim(k)
        return pltpu.make_async_remote_copy(
            src_ref=partial_out.at[to],
            dst_ref=sums.at[s_me * clips + c_me],
            send_sem=sem.at[2],
            recv_sem=sem.at[3],
            device_id=(c, s),
            device_id_type=MESH,
        )

    def start_sum(k, carry):
        @pl.when(aim(k)[0] != me)
        def _():
            send_sum(k).start()

        return carry

    lax.fori_loop(0, devices, start_sum, 0)
    sums[s_me * clips + c_me] = partial_out[me]

    def await_all(ref, at):
        others = ref.at[pl.ds(0, ref.shape[0] - 1)]
        pltpu.make_async_copy(others, others, sem.at[at]).wait()

    await_all(stats, 1)
    peaks = [stats[s, 0:1] for s in range(shards)]
    top = functools.reduce(jnp.maximum, peaks)
    lifts = [jnp.exp(p - top) for p in peaks]
    total = sum(stats[s, 1:2] * lifts[s] for s in range(shards))
    for s in range(shards):
        lift_out[s : s + 1] = lifts[s] / total
    lift[c_me] = lift_out[...]

    def send_lift(d):
        return pltpu.make_async_remote_copy(
            src_ref=lift_out,
            dst_ref=lift.at[c_me],
            send_sem=sem.at[6],
            recv_sem=sem.at[7],
            device_id=(lax.rem(c_me + d, clips), s_me),
            device_id_type=MESH,
        )

    for d in range(1, clips):
        send_lift(d).start()

    for i in range(CHUNKS):
        at = span(i)
        value = logits[at, :]
        weights = jnp.exp(value - jnp.max(value, axis=1, keepdims=True))
        combine[at, :] = (weights / jnp.sum(weights, axis=1, keepdims=True)).astype(BF16)

    await_all(lift, 7)
    lane = iota((2 * rows, slots), 1) == me * rows + iota((2 * rows, slots), 0) % rows
    own = [
        [
            jnp.sum(jnp.where(lane, lift[c, s : s + 1], 0.0), axis=1, keepdims=True)
            for s in range(shards)
        ]
        for c in range(clips)
    ]
    await_all(sums, 3)
    weighted = []
    for c in range(clips):
        value = jnp.zeros(sums.shape[1:], F32)
        for s in range(shards):
            value = value + sums[s * clips + c].astype(F32) * own[c][s]
        weighted.append(value[None])
    even, odd = (jnp.concatenate(weighted[p::2], axis=0) for p in range(2))
    wide = unspread(even, odd, rows).astype(BF16).astype(F32)

    mean = jnp.mean(wide * wide, axis=-1, keepdims=True)
    normalized = (wide * lax.rsqrt(mean + 1e-06)).astype(BF16)
    for load in weight_loads:
        load.wait()

    def mine(shape, expert):
        return (iota(shape, 0) % rows) // each == expert

    def choose(values):
        chosen = values[0]
        for e in range(1, experts):
            chosen = jnp.where(mine(chosen.shape, e), values[e], chosen)
        return chosen

    def spread_bias(ref, at):
        value = ref[:, at].astype(F32)
        size = (group, value.shape[1])
        return choose([jnp.broadcast_to(value[e : e + 1], size) for e in range(experts)])

    def expert_step(f, outs):
        at = pl.ds(pl.multiple_of(f * HIDDEN_CHUNK, HIDDEN_CHUNK), HIDDEN_CHUNK)
        before = choose([dot(normalized, w1_v[e, :, at]) for e in range(experts)])
        before = before + spread_bias(b1_v, at)
        hidden = (0.5 * before * (1.0 + lax.erf(before * math.sqrt(0.5)))).astype(BF16)
        return tuple(outs[e] + dot(hidden, w2_v[e, at, :]) for e in range(experts))

    outs = tuple(jnp.zeros((group, dim), F32) for _ in range(experts))
    outs = lax.fori_loop(0, ff // HIDDEN_CHUNK, expert_step, outs, unroll=True)
    result = (choose(outs) + spread_bias(b2_v, slice(None))).astype(BF16).astype(F32)
    even, odd = spread(result, rows)
    both = jnp.concatenate([even[:, None], odd[:, None]], axis=1).astype(BF16)
    back_out[...] = both.reshape(back_out.shape)

    def aim_back(k):
        c, s = lax.rem(k, clips), k // clips
        return c * shards + s, c, s

    def send_back(k):
        to, c, s = aim_back(k)
        return pltpu.make_async_remote_copy(
            src_ref=back_out.at[c],
            dst_ref=back_in.at[me],
            send_sem=sem.at[4],
            recv_sem=sem.at[5],
            device_id=(c, s),
            device_id_type=MESH,
        )

    def start_back(k, carry):
        @pl.when(aim_back(k)[0] != me)
        def _():
            send_back(k).start()

        return carry

    lax.fori_loop(0, devices, start_back, 0)
    back_in[me] = back_out[c_me]

    await_all(back_in, 5)
    value = back_in[...].astype(F32).reshape(pairs)
    returned[...] = unspread(value[:, 0], value[:, 1], rows).astype(BF16)
    await_all(stats, 0)
    await_all(sums, 2)
    await_all(back_in, 4)
    await_all(lift, 6)


def mix(combine, returned, mixed, buffer, sems):
    stores = []
    for i in range(combine.shape[0] // MIX_CHUNK):
        at = pl.ds(i * MIX_CHUNK, MIX_CHUNK)
        buffer[at, :] = dot(combine[at, :], returned[...]).astype(BF16)
        store = pltpu.make_async_copy(buffer.at[at], mixed.at[at], sems.at[i])
        store.start()
        stores.append(store)
    for store in stores:
        store.wait()


def local(clips, shards, tokens, scales, slot_params, w1, b1, w2, b2):
    count, dim = tokens.shape[1:]
    blocks = scales.shape[1]
    slots = slot_params.shape[1]
    rows = slots // (clips * shards)
    devices = clips * shards
    piece = (2 * rows, dim // 2)
    combine, returned = pl.pallas_call(
        functools.partial(kernel, clips, shards),
        out_shape=(pltpu.VMEM((count, slots), BF16), pltpu.VMEM((slots, dim), BF16)),
        in_specs=[pl.BlockSpec(memory_space=pltpu.HBM)] * 7,
        out_specs=(pl.BlockSpec(memory_space=pltpu.VMEM), pl.BlockSpec(memory_space=pltpu.VMEM)),
        scratch_shapes=[
            pltpu.VMEM((count, dim), BF16),
            pltpu.VMEM((blocks, 1, count), F32),
            pltpu.VMEM(slot_params.shape, BF16),
            pltpu.VMEM(w1.shape, BF16),
            pltpu.VMEM(b1.shape, BF16),
            pltpu.VMEM(w2.shape, BF16),
            pltpu.VMEM(b2.shape, BF16),
            pltpu.VMEM((count, slots), F32),
            pltpu.VMEM((count, slots), BF16),
            pltpu.VMEM((2, slots), F32),
            pltpu.VMEM((shards, 2, slots), F32),
            pltpu.VMEM((shards, slots), F32),
            pltpu.VMEM((clips, shards, slots), F32),
            pltpu.VMEM((devices,) + piece, BF16),
            pltpu.VMEM((devices,) + piece, BF16),
            pltpu.VMEM((clips,) + piece, BF16),
            pltpu.VMEM((devices,) + piece, BF16),
            pltpu.SemaphoreType.DMA((6,)),
            pltpu.SemaphoreType.DMA((CHUNKS,)),
            pltpu.SemaphoreType.DMA((8,)),
        ],
        compiler_params=pltpu.CompilerParams(
            collective_id=0, has_side_effects=True, vmem_limit_bytes=57 << 20
        ),
        name="slots",
    )(tokens[0], scales.transpose(1, 0, 2), slot_params, w1, b1, w2, b2)
    mixed = pl.pallas_call(
        mix,
        out_shape=jax.ShapeDtypeStruct((count, dim), BF16),
        in_specs=[pl.BlockSpec(memory_space=pltpu.VMEM)] * 2,
        out_specs=pl.BlockSpec(memory_space=pl.ANY),
        scratch_shapes=[
            pltpu.VMEM((count, dim), BF16),
            pltpu.SemaphoreType.DMA((count // MIX_CHUNK,)),
        ],
        compiler_params=pltpu.CompilerParams(vmem_limit_bytes=16 << 20),
        name="mix",
    )(combine, returned)
    return mixed[None]


def solution(mesh):
    placed = (
        P("clip", "shard", None),
        P("clip", None, "shard"),
        P(),
        P(("clip", "shard"), None, None),
        P(("clip", "shard"), None),
        P(("clip", "shard"), None, None),
        P(("clip", "shard"), None),
    )
    return jax.shard_map(
        functools.partial(local, mesh.shape["clip"], mesh.shape["shard"]),
        mesh=mesh,
        in_specs=placed,
        out_specs=P("clip", "shard", None),
        check_vma=False,
    )
```

```python
import functools
import math

import jax
import jax.numpy as jnp
from jax import lax
from jax.experimental import pallas as pl
from jax.experimental.pallas import tpu as pltpu
from jax.sharding import PartitionSpec as P

F32 = jnp.float32
BF16 = jnp.bfloat16
MESH = pl.DeviceIdType.MESH
CHUNKS = 2
MIX_CHUNK = 256
HIDDEN_CHUNK = 768
LANES = 128
TILE = 8


def dot(a, b, contract=((1,), (0,))):
    return lax.dot_general(a, b, (contract, ((), ())), preferred_element_type=F32)


def iota(shape, axis):
    return lax.broadcasted_iota(jnp.int32, shape, axis)


def kernel(
    clips,
    shards,
    tokens,
    scales,
    slot_params,
    w1,
    b1,
    w2,
    b2,
    combine,
    returned,
    feat,
    scale_v,
    params_v,
    w1_v,
    b1_v,
    w2_v,
    b2_v,
    logits,
    lifted,
    stats_out,
    stats,
    lift_out,
    lift,
    packed,
    sum_out_a,
    sum_out_b,
    sum_in_a,
    sum_in_b,
    sum_a,
    sum_b,
    back_packed,
    back_out_a,
    back_out_b,
    back_in_a,
    back_in_b,
    back_a,
    back_b,
    local_sem,
    token_sem,
    weight_sem,
    sem,
):
    c_me, s_me = lax.axis_index("clip"), lax.axis_index("shard")
    count, dim = feat.shape
    blocks = scale_v.shape[0]
    width = dim // blocks
    slots = params_v.shape[1]
    experts, _, ff = w1_v.shape
    devices = clips * shards
    rows = slots // devices
    each = rows // experts
    parts = dim // LANES
    sub = rows * parts
    send_cut = sum_in_a.shape[1]
    back_cut = back_in_a.shape[1]
    me = c_me * shards + s_me
    chunk = count // CHUNKS

    def span(i):
        return pl.ds(i * chunk, chunk)

    load_scale = pltpu.make_async_copy(scales, scale_v, local_sem.at[0])
    load_params = pltpu.make_async_copy(slot_params, params_v, local_sem.at[1])
    load_params.start()
    load_scale.start()
    for i in range(CHUNKS):
        pltpu.make_async_copy(tokens.at[span(i)], feat.at[span(i)], token_sem.at[i]).start()
    bias_loads = [
        pltpu.make_async_copy(b1, b1_v, local_sem.at[2]),
        pltpu.make_async_copy(b2, b2_v, local_sem.at[3]),
    ]
    weight_loads = [
        [
            pltpu.make_async_copy(w1.at[e], w1_v.at[e], weight_sem.at[e, 0]),
            pltpu.make_async_copy(w2.at[e], w2_v.at[e], weight_sem.at[e, 1]),
        ]
        for e in range(experts)
    ]
    barrier = pltpu.get_barrier_semaphore()

    def greet(d, carry):
        at = lax.rem(me + d, devices)
        to = (at // shards, lax.rem(at, shards))
        pl.semaphore_signal(barrier, inc=1, device_id=to, device_id_type=MESH)
        return carry

    lax.fori_loop(1, devices, greet, 0)
    load_params.wait()
    here, there = iota((slots, slots), 0), iota((slots, slots), 1)
    order = (here // rows == there % devices) & (here % rows == there // devices)
    params = dot(params_v[...], jnp.where(order, 1.0, 0.0).astype(BF16)).astype(BF16)
    load_scale.wait()

    peak = jnp.full((1, slots), -jnp.inf, F32)
    for i in range(CHUNKS):
        at = span(i)
        pltpu.make_async_copy(tokens.at[at], feat.at[at], token_sem.at[i]).wait()
        if i == CHUNKS - 1:
            for load in bias_loads:
                load.start()
            for pair in weight_loads:
                for load in pair:
                    load.start()
        scaled = jnp.concatenate(
            [
                feat[at, b * width : (b + 1) * width].astype(F32)
                * jnp.broadcast_to(scale_v[b, 0:1, at], (width, chunk)).T
                for b in range(blocks)
            ],
            axis=1,
        ).astype(BF16)
        feat[at, :] = scaled
        value = dot(scaled, params)
        logits[at, :] = value
        peak = jnp.maximum(peak, jnp.max(value, axis=0, keepdims=True))

    total = jnp.zeros((1, slots), F32)
    for i in range(CHUNKS):
        at = span(i)
        value = jnp.exp(logits[at, :] - peak)
        total = total + jnp.sum(value, axis=0, keepdims=True)
        lifted[at, :] = value.astype(BF16)
    stats_out[0:1, :] = peak
    stats_out[1:2, :] = total
    stats[s_me] = stats_out[...]
    pl.semaphore_wait(barrier, devices - 1)

    def send(src, dst, at, c, s):
        return pltpu.make_async_remote_copy(
            src_ref=src,
            dst_ref=dst,
            send_sem=sem.at[2 * at],
            recv_sem=sem.at[2 * at + 1],
            device_id=(c, s),
            device_id_type=MESH,
        )

    def await_all(ref, at):
        others = ref.at[pl.ds(0, ref.shape[0] - 1)]
        pltpu.make_async_copy(others, others, sem.at[at]).wait()

    for d in range(1, shards):
        send(stats_out, stats.at[s_me], 0, c_me, lax.rem(s_me + d, shards)).start()

    partial = dot(lifted[...], feat[...], ((0,), (0,)))
    for r in range(rows):
        for b in range(parts):
            packed[pl.ds(r * parts + b, devices, stride=sub), :] = partial[
                r * devices : (r + 1) * devices, b * LANES : (b + 1) * LANES
            ]
    both = packed[...].reshape(devices, sub, LANES).astype(BF16)
    sum_out_a[...] = both[:, :send_cut]
    sum_out_b[...] = both[:, send_cut:]

    mine = s_me * clips + c_me
    for at, out, landing in ((1, sum_out_a, sum_in_a), (2, sum_out_b, sum_in_b)):
        for s in range(shards):
            for i in range(clips):
                c = lax.rem(c_me + i, clips)
                copy = send(out.at[c * shards + s], landing.at[mine], at, c, s)
                if i == 0:
                    pl.when(s_me != s)(copy.start)
                else:
                    copy.start()
    sum_in_a[mine] = sum_out_a[me]
    sum_in_b[mine] = sum_out_b[me]

    await_all(stats, 1)
    peaks = [stats[s, 0:1] for s in range(shards)]
    top = functools.reduce(jnp.maximum, peaks)
    lifts = [jnp.exp(p - top) for p in peaks]
    total = sum(stats[s, 1:2] * lifts[s] for s in range(shards))
    for s in range(shards):
        lift_out[s : s + 1] = lifts[s] / total
    lift[c_me] = lift_out[...]
    for d in range(1, clips):
        send(lift_out, lift.at[c_me], 3, lax.rem(c_me + d, clips), s_me).start()

    for i in range(CHUNKS):
        at = span(i)
        value = logits[at, :]
        weights = jnp.exp(value - jnp.max(value, axis=1, keepdims=True))
        combine[at, :] = (weights / jnp.sum(weights, axis=1, keepdims=True)).astype(BF16)

    await_all(lift, 7)
    lane = iota((clips, slots), 1)
    own = [
        [
            jnp.sum(
                jnp.where(lane == r * devices + me, lift[:, s, :], 0.0), axis=1, keepdims=True
            )
            for r in range(rows)
        ]
        for s in range(shards)
    ]

    def strip(low, high, cut, i, base, size):
        if i < cut:
            return low[pl.ds(base * cut + i, size, stride=cut), :]
        return high[pl.ds(base * (sub - cut) + i - cut, size, stride=sub - cut), :]

    def slot_rows(r):
        strips = []
        for b in range(parts):
            i = r * parts + b
            terms = [
                strip(sum_a, sum_b, send_cut, i, s * clips, clips) * own[s][r]
                for s in range(shards)
            ]
            strips.append(sum(terms[1:], terms[0]))
        return jnp.concatenate(strips, axis=1)

    def expert(e):
        wide = jnp.concatenate([slot_rows(e * each + q) for q in range(each)], axis=0)
        wide = wide.astype(BF16).astype(F32)
        mean = jnp.mean(wide * wide, axis=-1, keepdims=True)
        normalized = (wide * lax.rsqrt(mean + 1e-06)).astype(BF16)
        for load in weight_loads[e]:
            load.wait()
        out = b2_v[...].astype(F32)[e : e + 1]
        for f in range(ff // HIDDEN_CHUNK):
            at = slice(f * HIDDEN_CHUNK, (f + 1) * HIDDEN_CHUNK)
            before = dot(normalized, w1_v[e, :, at]) + b1_v[:, at].astype(F32)[e : e + 1]
            hidden = (0.5 * before * (1.0 + lax.erf(before * math.sqrt(0.5)))).astype(BF16)
            out = out + dot(hidden, w2_v[e, at, :])
        out = out.astype(BF16).astype(F32)
        for q in range(each):
            for b in range(parts):
                i = (e * each + q) * parts + b
                back_packed[pl.ds(i, clips, stride=sub), :] = out[
                    q * clips : (q + 1) * clips, b * LANES : (b + 1) * LANES
                ]

    def back(at, c, s):
        out, landing = (back_out_a, back_in_a) if at == 4 else (back_out_b, back_in_b)
        return send(out.at[c], landing.at[me], at, c, s)

    def send_back(at, s):
        for c in range(clips):
            pl.when(me != c * shards + s)(back(at, c, s).start)

    for load in bias_loads:
        load.wait()
    await_all(sum_in_a, 3)
    sum_a[...] = sum_in_a[...].astype(F32).reshape(sum_a.shape)
    expert(0)
    for c in range(clips):
        back_out_a[c] = back_packed[pl.ds(c * sub, back_cut), :].astype(BF16)
    send_back(4, 0)
    await_all(sum_in_b, 5)
    sum_b[...] = sum_in_b[...].astype(F32).reshape(sum_b.shape)
    for e in range(1, experts):
        expert(e)
    for c in range(clips):
        back_out_b[c] = back_packed[pl.ds(c * sub + back_cut, sub - back_cut), :].astype(BF16)
    send_back(5, 0)
    for s in range(1, shards):
        send_back(4, s)
        send_back(5, s)
    back_in_a[me] = back_out_a[c_me]
    back_in_b[me] = back_out_b[c_me]

    for at, landing, flat in ((9, back_in_a, back_a), (11, back_in_b, back_b)):
        await_all(landing, at)
        flat[...] = landing[...].astype(F32).reshape(flat.shape)
    for r in range(rows):
        for b in range(parts):
            value = strip(back_a, back_b, back_cut, r * parts + b, 0, devices)
            returned[r * devices : (r + 1) * devices, b * LANES : (b + 1) * LANES] = value.astype(BF16)
    for ref, at in (
        (stats, 0),
        (sum_in_a, 2),
        (sum_in_b, 4),
        (lift, 6),
        (back_in_a, 8),
        (back_in_b, 10),
    ):
        await_all(ref, at)


def mix(combine, returned, mixed, buffer, sems):
    stores = []
    for i in range(combine.shape[0] // MIX_CHUNK):
        at = pl.ds(i * MIX_CHUNK, MIX_CHUNK)
        buffer[at, :] = dot(combine[at, :], returned[...]).astype(BF16)
        store = pltpu.make_async_copy(buffer.at[at], mixed.at[at], sems.at[i])
        store.start()
        stores.append(store)
    for store in stores:
        store.wait()


def local(clips, shards, tokens, scales, slot_params, w1, b1, w2, b2):
    count, dim = tokens.shape[1:]
    blocks = scales.shape[1]
    slots = slot_params.shape[1]
    devices = clips * shards
    parts = dim // LANES
    sub = slots // devices * parts
    half = sub // w1.shape[0]
    send_cut = -(-half // TILE) * TILE
    back_cut = half // TILE * TILE

    def pieces(number, cut, dtype):
        if dtype == F32:
            return [pltpu.VMEM((number * n, LANES), F32) for n in (cut, sub - cut)]
        return [pltpu.VMEM((number, n, LANES), dtype) for n in (cut, sub - cut)]

    combine, returned = pl.pallas_call(
        functools.partial(kernel, clips, shards),
        out_shape=(pltpu.VMEM((count, slots), BF16), pltpu.VMEM((slots, dim), BF16)),
        in_specs=[pl.BlockSpec(memory_space=pltpu.HBM)] * 7,
        out_specs=(pl.BlockSpec(memory_space=pltpu.VMEM), pl.BlockSpec(memory_space=pltpu.VMEM)),
        scratch_shapes=[
            pltpu.VMEM((count, dim), BF16),
            pltpu.VMEM((blocks, 1, count), F32),
            pltpu.VMEM(slot_params.shape, BF16),
            pltpu.VMEM(w1.shape, BF16),
            pltpu.VMEM(b1.shape, BF16),
            pltpu.VMEM(w2.shape, BF16),
            pltpu.VMEM(b2.shape, BF16),
            pltpu.VMEM((count, slots), F32),
            pltpu.VMEM((count, slots), BF16),
            pltpu.VMEM((2, slots), F32),
            pltpu.VMEM((shards, 2, slots), F32),
            pltpu.VMEM((shards, slots), F32),
            pltpu.VMEM((clips, shards, slots), F32),
            pltpu.VMEM((devices * sub, LANES), F32),
            *pieces(devices, send_cut, BF16),
            *pieces(devices, send_cut, BF16),
            *pieces(devices, send_cut, F32),
            pltpu.VMEM((clips * sub, LANES), F32),
            *pieces(clips, back_cut, BF16),
            *pieces(devices, back_cut, BF16),
            *pieces(devices, back_cut, F32),
            pltpu.SemaphoreType.DMA((4,)),
            pltpu.SemaphoreType.DMA((CHUNKS,)),
            pltpu.SemaphoreType.DMA((w1.shape[0], 2)),
            pltpu.SemaphoreType.DMA((12,)),
        ],
        compiler_params=pltpu.CompilerParams(
            collective_id=0, has_side_effects=True, vmem_limit_bytes=57 << 20
        ),
        name="slots",
    )(tokens[0], scales.transpose(1, 0, 2), slot_params, w1, b1, w2, b2)
    mixed = pl.pallas_call(
        mix,
        out_shape=jax.ShapeDtypeStruct((count, dim), BF16),
        in_specs=[pl.BlockSpec(memory_space=pltpu.VMEM)] * 2,
        out_specs=pl.BlockSpec(memory_space=pl.ANY),
        scratch_shapes=[
            pltpu.VMEM((count, dim), BF16),
            pltpu.SemaphoreType.DMA((count // MIX_CHUNK,)),
        ],
        compiler_params=pltpu.CompilerParams(vmem_limit_bytes=16 << 20),
        name="mix",
    )(combine, returned)
    return mixed[None]


def solution(mesh):
    placed = (
        P("clip", "shard", None),
        P("clip", None, "shard"),
        P(),
        P(("clip", "shard"), None, None),
        P(("clip", "shard"), None),
        P(("clip", "shard"), None, None),
        P(("clip", "shard"), None),
    )
    return jax.shard_map(
        functools.partial(local, mesh.shape["clip"], mesh.shape["shard"]),
        mesh=mesh,
        in_specs=placed,
        out_specs=P("clip", "shard", None),
        check_vma=False,
    )
```

```python
import functools
import math

import jax
import jax.numpy as jnp
from jax import lax
from jax.experimental import pallas as pl
from jax.experimental.pallas import tpu as pltpu
from jax.sharding import PartitionSpec as P

F32 = jnp.float32
BF16 = jnp.bfloat16
MESH = pl.DeviceIdType.MESH
CHUNKS = 2
MIX_CHUNK = 256
HIDDEN_CHUNK = 1536
LANES = 128
TILE = 8


def dot(a, b, contract=((1,), (0,))):
    return lax.dot_general(a, b, (contract, ((), ())), preferred_element_type=F32)


def iota(shape, axis):
    return lax.broadcasted_iota(jnp.int32, shape, axis)


def kernel(
    clips,
    shards,
    tokens,
    scales,
    slot_params,
    w1,
    b1,
    w2,
    b2,
    combine,
    returned,
    feat,
    scale_v,
    params_v,
    w1_v,
    b1_v,
    w2_v,
    b2_v,
    logits,
    lifted,
    stats_out,
    stats,
    lift_out,
    lift,
    sum_out_a,
    sum_out_b,
    sum_in_a,
    sum_in_b,
    sum_a,
    sum_b,
    back_packed,
    back_out_a,
    back_out_b,
    back_in_a,
    back_in_b,
    back_a,
    back_b,
    local_sem,
    token_sem,
    weight_sem,
    sem,
):
    c_me, s_me = lax.axis_index("clip"), lax.axis_index("shard")
    count, dim = feat.shape
    blocks = scale_v.shape[0]
    width = dim // blocks
    slots = params_v.shape[1]
    experts, _, ff = w1_v.shape
    devices = clips * shards
    rows = slots // devices
    each = rows // experts
    parts = dim // LANES
    sub = rows * parts
    send_cut = sum_in_a.shape[1]
    back_cut = back_in_a.shape[1]
    me = c_me * shards + s_me
    chunk = count // CHUNKS

    def span(i):
        return pl.ds(i * chunk, chunk)

    load_scale = pltpu.make_async_copy(scales, scale_v, local_sem.at[0])
    load_params = pltpu.make_async_copy(slot_params, params_v, local_sem.at[1])
    load_params.start()
    load_scale.start()
    for i in range(CHUNKS):
        pltpu.make_async_copy(tokens.at[span(i)], feat.at[span(i)], token_sem.at[i]).start()
    bias_loads = [
        pltpu.make_async_copy(b1, b1_v, local_sem.at[2]),
        pltpu.make_async_copy(b2, b2_v, local_sem.at[3]),
    ]
    weight_loads = [
        [
            pltpu.make_async_copy(w1.at[e], w1_v.at[e], weight_sem.at[e, 0]),
            pltpu.make_async_copy(w2.at[e], w2_v.at[e], weight_sem.at[e, 1]),
        ]
        for e in range(experts)
    ]
    barrier = pltpu.get_barrier_semaphore()

    def greet(d, carry):
        at = lax.rem(me + d, devices)
        to = (at // shards, lax.rem(at, shards))
        pl.semaphore_signal(barrier, inc=1, device_id=to, device_id_type=MESH)
        return carry

    lax.fori_loop(1, devices, greet, 0)
    load_params.wait()
    here, there = iota((slots, slots), 0), iota((slots, slots), 1)
    order = (here // rows == there % devices) & (here % rows == there // devices)
    params = dot(params_v[...], jnp.where(order, 1.0, 0.0).astype(BF16)).astype(BF16)
    load_scale.wait()

    def scale_rows(i):
        at = span(i)
        feat[at, :] = jnp.concatenate(
            [
                feat[at, b * width : (b + 1) * width].astype(F32)
                * jnp.broadcast_to(scale_v[b, 0:1, at], (width, chunk)).T
                for b in range(blocks)
            ],
            axis=1,
        ).astype(BF16)

    def score(i, peak):
        value = dot(feat[span(i), :], params)
        logits[span(i), :] = value
        return jnp.maximum(peak, jnp.max(value, axis=0, keepdims=True))

    peak = jnp.full((1, slots), -jnp.inf, F32)
    for i in range(CHUNKS):
        at = span(i)
        pltpu.make_async_copy(tokens.at[at], feat.at[at], token_sem.at[i]).wait()
        if i == CHUNKS - 1:
            for load in bias_loads:
                load.start()
            for pair in weight_loads:
                for load in pair:
                    load.start()
        if i > 0:
            peak = score(i - 1, peak)
        scale_rows(i)
    peak = score(CHUNKS - 1, peak)

    total = jnp.zeros((1, slots), F32)
    for i in range(CHUNKS):
        at = span(i)
        value = jnp.exp(logits[at, :] - peak)
        total = total + jnp.sum(value, axis=0, keepdims=True)
        lifted[at, :] = value.astype(BF16)
    stats_out[0:1, :] = peak
    stats_out[1:2, :] = total
    stats[s_me] = stats_out[...]
    pl.semaphore_wait(barrier, devices - 1)

    def send(src, dst, at, c, s):
        return pltpu.make_async_remote_copy(
            src_ref=src,
            dst_ref=dst,
            send_sem=sem.at[2 * at],
            recv_sem=sem.at[2 * at + 1],
            device_id=(c, s),
            device_id_type=MESH,
        )

    def await_all(ref, at):
        others = ref.at[pl.ds(0, ref.shape[0] - 1)]
        pltpu.make_async_copy(others, others, sem.at[at]).wait()

    for d in range(1, shards):
        send(stats_out, stats.at[s_me], 0, c_me, lax.rem(s_me + d, shards)).start()

    partial = dot(lifted[...], feat[...], ((0,), (0,)))
    mine = s_me * clips + c_me
    for at, flat, out, landing, first in (
        (1, sum_a, sum_out_a, sum_in_a, 0),
        (2, sum_b, sum_out_b, sum_in_b, send_cut),
    ):
        size = out.shape[1]
        for i in range(size):
            r, b = divmod(first + i, parts)
            flat[pl.ds(i, devices, stride=size), :] = partial[
                r * devices : (r + 1) * devices, b * LANES : (b + 1) * LANES
            ]
        out[...] = flat[...].reshape(out.shape).astype(BF16)
        for s in range(shards):
            for i in range(clips):
                c = lax.rem(c_me + i, clips)
                copy = send(out.at[c * shards + s], landing.at[mine], at, c, s)
                if i == 0:
                    pl.when(s_me != s)(copy.start)
                else:
                    copy.start()
    sum_in_a[mine] = sum_out_a[me]
    sum_in_b[mine] = sum_out_b[me]

    await_all(stats, 1)
    peaks = [stats[s, 0:1] for s in range(shards)]
    top = functools.reduce(jnp.maximum, peaks)
    lifts = [jnp.exp(p - top) for p in peaks]
    total = sum(stats[s, 1:2] * lifts[s] for s in range(shards))
    for s in range(shards):
        lift_out[s : s + 1] = lifts[s] / total
    lift[c_me] = lift_out[...]
    for d in range(1, clips):
        send(lift_out, lift.at[c_me], 3, lax.rem(c_me + d, clips), s_me).start()

    for i in range(CHUNKS):
        at = span(i)
        value = logits[at, :]
        weights = jnp.exp(value - jnp.max(value, axis=1, keepdims=True))
        combine[at, :] = (weights / jnp.sum(weights, axis=1, keepdims=True)).astype(BF16)

    await_all(lift, 7)
    lane = iota((clips, slots), 1)
    own = [
        [
            jnp.sum(
                jnp.where(lane == r * devices + me, lift[:, s, :], 0.0), axis=1, keepdims=True
            )
            for r in range(rows)
        ]
        for s in range(shards)
    ]

    def strip(low, high, cut, i, base, size):
        if i < cut:
            return low[pl.ds(base * cut + i, size, stride=cut), :]
        return high[pl.ds(base * (sub - cut) + i - cut, size, stride=sub - cut), :]

    def slot_rows(r):
        strips = []
        for b in range(parts):
            i = r * parts + b
            terms = [
                strip(sum_a, sum_b, send_cut, i, s * clips, clips) * own[s][r]
                for s in range(shards)
            ]
            strips.append(sum(terms[1:], terms[0]))
        return jnp.concatenate(strips, axis=1)

    def expert(e):
        wide = jnp.concatenate([slot_rows(e * each + q) for q in range(each)], axis=0)
        wide = wide.astype(BF16).astype(F32)
        mean = jnp.mean(wide * wide, axis=-1, keepdims=True)
        normalized = (wide * lax.rsqrt(mean + 1e-06)).astype(BF16)
        for load in weight_loads[e]:
            load.wait()
        out = b2_v[...].astype(F32)[e : e + 1]
        for f in range(ff // HIDDEN_CHUNK):
            at = slice(f * HIDDEN_CHUNK, (f + 1) * HIDDEN_CHUNK)
            before = dot(normalized, w1_v[e, :, at]) + b1_v[:, at].astype(F32)[e : e + 1]
            hidden = (0.5 * before * (1.0 + lax.erf(before * math.sqrt(0.5)))).astype(BF16)
            out = out + dot(hidden, w2_v[e, at, :])
        out = out.astype(BF16).astype(F32)
        for q in range(each):
            for b in range(parts):
                i = (e * each + q) * parts + b
                back_packed[pl.ds(i, clips, stride=sub), :] = out[
                    q * clips : (q + 1) * clips, b * LANES : (b + 1) * LANES
                ]

    def back(at, c, s):
        out, landing = (back_out_a, back_in_a) if at == 4 else (back_out_b, back_in_b)
        return send(out.at[c], landing.at[me], at, c, s)

    def send_back(at, s):
        for c in range(clips):
            pl.when(me != c * shards + s)(back(at, c, s).start)

    for load in bias_loads:
        load.wait()
    await_all(sum_in_a, 3)
    sum_a[...] = sum_in_a[...].astype(F32).reshape(sum_a.shape)
    expert(0)
    for c in range(clips):
        back_out_a[c] = back_packed[pl.ds(c * sub, back_cut), :].astype(BF16)
    send_back(4, 0)
    await_all(sum_in_b, 5)
    sum_b[...] = sum_in_b[...].astype(F32).reshape(sum_b.shape)
    for e in range(1, experts):
        expert(e)
    for c in range(clips):
        back_out_b[c] = back_packed[pl.ds(c * sub + back_cut, sub - back_cut), :].astype(BF16)
    send_back(5, 0)
    for s in range(1, shards):
        send_back(4, s)
        send_back(5, s)
    back_in_a[me] = back_out_a[c_me]
    back_in_b[me] = back_out_b[c_me]

    for at, landing, flat, first in (
        (9, back_in_a, back_a, 0),
        (11, back_in_b, back_b, back_cut),
    ):
        size = landing.shape[1]
        await_all(landing, at)
        flat[...] = landing[...].astype(F32).reshape(flat.shape)
        for i in range(size):
            r, b = divmod(first + i, parts)
            returned[r * devices : (r + 1) * devices, b * LANES : (b + 1) * LANES] = flat[
                pl.ds(i, devices, stride=size), :
            ].astype(BF16)
    for ref, at in (
        (stats, 0),
        (sum_in_a, 2),
        (sum_in_b, 4),
        (lift, 6),
        (back_in_a, 8),
        (back_in_b, 10),
    ):
        await_all(ref, at)


def mix(combine, returned, mixed, buffer, sems):
    stores = []
    for i in range(combine.shape[0] // MIX_CHUNK):
        at = pl.ds(i * MIX_CHUNK, MIX_CHUNK)
        buffer[at, :] = dot(combine[at, :], returned[...]).astype(BF16)
        store = pltpu.make_async_copy(buffer.at[at], mixed.at[at], sems.at[i])
        store.start()
        stores.append(store)
    for store in stores:
        store.wait()


def local(clips, shards, tokens, scales, slot_params, w1, b1, w2, b2):
    count, dim = tokens.shape[1:]
    blocks = scales.shape[1]
    slots = slot_params.shape[1]
    devices = clips * shards
    parts = dim // LANES
    sub = slots // devices * parts
    half = sub // w1.shape[0]
    send_cut = -(-half // TILE) * TILE
    back_cut = half // TILE * TILE

    def pieces(number, cut, dtype):
        if dtype == F32:
            return [pltpu.VMEM((number * n, LANES), F32) for n in (cut, sub - cut)]
        return [pltpu.VMEM((number, n, LANES), dtype) for n in (cut, sub - cut)]

    combine, returned = pl.pallas_call(
        functools.partial(kernel, clips, shards),
        out_shape=(pltpu.VMEM((count, slots), BF16), pltpu.VMEM((slots, dim), BF16)),
        in_specs=[pl.BlockSpec(memory_space=pltpu.HBM)] * 7,
        out_specs=(pl.BlockSpec(memory_space=pltpu.VMEM), pl.BlockSpec(memory_space=pltpu.VMEM)),
        scratch_shapes=[
            pltpu.VMEM((count, dim), BF16),
            pltpu.VMEM((blocks, 1, count), F32),
            pltpu.VMEM(slot_params.shape, BF16),
            pltpu.VMEM(w1.shape, BF16),
            pltpu.VMEM(b1.shape, BF16),
            pltpu.VMEM(w2.shape, BF16),
            pltpu.VMEM(b2.shape, BF16),
            pltpu.VMEM((count, slots), F32),
            pltpu.VMEM((count, slots), BF16),
            pltpu.VMEM((2, slots), F32),
            pltpu.VMEM((shards, 2, slots), F32),
            pltpu.VMEM((shards, slots), F32),
            pltpu.VMEM((clips, shards, slots), F32),
            *pieces(devices, send_cut, BF16),
            *pieces(devices, send_cut, BF16),
            *pieces(devices, send_cut, F32),
            pltpu.VMEM((clips * sub, LANES), F32),
            *pieces(clips, back_cut, BF16),
            *pieces(devices, back_cut, BF16),
            *pieces(devices, back_cut, F32),
            pltpu.SemaphoreType.DMA((4,)),
            pltpu.SemaphoreType.DMA((CHUNKS,)),
            pltpu.SemaphoreType.DMA((w1.shape[0], 2)),
            pltpu.SemaphoreType.DMA((12,)),
        ],
        compiler_params=pltpu.CompilerParams(
            collective_id=0, has_side_effects=True, vmem_limit_bytes=57 << 20
        ),
        name="slots",
    )(tokens[0], scales.transpose(1, 0, 2), slot_params, w1, b1, w2, b2)
    mixed = pl.pallas_call(
        mix,
        out_shape=jax.ShapeDtypeStruct((count, dim), BF16),
        in_specs=[pl.BlockSpec(memory_space=pltpu.VMEM)] * 2,
        out_specs=pl.BlockSpec(memory_space=pl.ANY),
        scratch_shapes=[
            pltpu.VMEM((count, dim), BF16),
            pltpu.SemaphoreType.DMA((count // MIX_CHUNK,)),
        ],
        compiler_params=pltpu.CompilerParams(vmem_limit_bytes=16 << 20),
        name="mix",
    )(combine, returned)
    return mixed[None]


def solution(mesh):
    placed = (
        P("clip", "shard", None),
        P("clip", None, "shard"),
        P(),
        P(("clip", "shard"), None, None),
        P(("clip", "shard"), None),
        P(("clip", "shard"), None, None),
        P(("clip", "shard"), None),
    )
    return jax.shard_map(
        functools.partial(local, mesh.shape["clip"], mesh.shape["shard"]),
        mesh=mesh,
        in_specs=placed,
        out_specs=P("clip", "shard", None),
        check_vma=False,
    )
```

```python
import functools
import math

import jax
import jax.numpy as jnp
from jax import lax
from jax.experimental import pallas as pl
from jax.experimental.pallas import tpu as pltpu
from jax.sharding import PartitionSpec as P

F32 = jnp.float32
BF16 = jnp.bfloat16
MESH = pl.DeviceIdType.MESH
CHUNKS = 2
MIX_CHUNK = 256
HIDDEN_CHUNK = 1536
LANES = 128
TILE = 8


def dot(a, b, contract=((1,), (0,))):
    return lax.dot_general(a, b, (contract, ((), ())), preferred_element_type=F32)


def iota(shape, axis):
    return lax.broadcasted_iota(jnp.int32, shape, axis)


def kernel(
    clips,
    shards,
    tokens,
    scales,
    slot_params,
    w1,
    b1,
    w2,
    b2,
    combine,
    returned,
    feat,
    scale_v,
    params_v,
    w1_v,
    b1_v,
    w2_v,
    b2_v,
    logits,
    lifted,
    stats_out,
    stats,
    lift_out,
    lift,
    sum_out_a,
    sum_out_b,
    sum_in_a,
    sum_in_b,
    sum_a,
    sum_b,
    back_packed,
    back_out_a,
    back_out_b,
    back_in_a,
    back_in_b,
    back_a,
    back_b,
    local_sem,
    token_sem,
    weight_sem,
    sem,
):
    c_me, s_me = lax.axis_index("clip"), lax.axis_index("shard")
    count, dim = feat.shape
    blocks = scale_v.shape[0]
    width = dim // blocks
    slots = params_v.shape[1]
    experts, _, ff = w1_v.shape
    devices = clips * shards
    rows = slots // devices
    each = rows // experts
    parts = dim // LANES
    sub = rows * parts
    send_cut = sum_in_a.shape[1]
    back_cut = back_in_a.shape[1]
    me = c_me * shards + s_me
    chunk = count // CHUNKS

    def span(i):
        return pl.ds(i * chunk, chunk)

    load_scale = pltpu.make_async_copy(scales, scale_v, local_sem.at[0])
    load_params = pltpu.make_async_copy(slot_params, params_v, local_sem.at[1])
    load_params.start()
    load_scale.start()
    for i in range(CHUNKS):
        pltpu.make_async_copy(tokens.at[span(i)], feat.at[span(i)], token_sem.at[i]).start()
    bias_loads = [
        pltpu.make_async_copy(b1, b1_v, local_sem.at[2]),
        pltpu.make_async_copy(b2, b2_v, local_sem.at[3]),
    ]
    weight_loads = [
        [
            pltpu.make_async_copy(w1.at[e], w1_v.at[e], weight_sem.at[e, 0]),
            pltpu.make_async_copy(w2.at[e], w2_v.at[e], weight_sem.at[e, 1]),
        ]
        for e in range(experts)
    ]
    barrier = pltpu.get_barrier_semaphore()

    def greet(d, carry):
        at = lax.rem(me + d, devices)
        to = (at // shards, lax.rem(at, shards))
        pl.semaphore_signal(barrier, inc=1, device_id=to, device_id_type=MESH)
        return carry

    lax.fori_loop(1, devices, greet, 0)
    load_params.wait()
    here, there = iota((slots, slots), 0), iota((slots, slots), 1)
    order = (here // rows == there % devices) & (here % rows == there // devices)
    params = dot(params_v[...], jnp.where(order, 1.0, 0.0).astype(BF16)).astype(BF16)
    load_scale.wait()

    def scale_rows(i):
        at = span(i)
        feat[at, :] = jnp.concatenate(
            [
                feat[at, b * width : (b + 1) * width].astype(F32)
                * jnp.broadcast_to(scale_v[b, 0:1, at], (width, chunk)).T
                for b in range(blocks)
            ],
            axis=1,
        ).astype(BF16)

    def score(i, peak):
        value = dot(feat[span(i), :], params)
        logits[span(i), :] = value
        return jnp.maximum(peak, jnp.max(value, axis=0, keepdims=True))

    peak = jnp.full((1, slots), -jnp.inf, F32)
    for i in range(CHUNKS):
        at = span(i)
        pltpu.make_async_copy(tokens.at[at], feat.at[at], token_sem.at[i]).wait()
        if i == CHUNKS - 1:
            for load in bias_loads:
                load.start()
            for pair in weight_loads:
                for load in pair:
                    load.start()
        if i > 0:
            peak = score(i - 1, peak)
        scale_rows(i)
    peak = score(CHUNKS - 1, peak)

    total = jnp.zeros((1, slots), F32)
    for i in range(CHUNKS):
        at = span(i)
        value = jnp.exp(logits[at, :] - peak)
        total = total + jnp.sum(value, axis=0, keepdims=True)
        lifted[at, :] = value.astype(BF16)
    stats_out[0:1, :] = peak
    stats_out[1:2, :] = total
    stats[s_me] = stats_out[...]
    pl.semaphore_wait(barrier, devices - 1)

    def send(src, dst, at, c, s):
        return pltpu.make_async_remote_copy(
            src_ref=src,
            dst_ref=dst,
            send_sem=sem.at[2 * at],
            recv_sem=sem.at[2 * at + 1],
            device_id=(c, s),
            device_id_type=MESH,
        )

    def await_all(ref, at):
        others = ref.at[pl.ds(0, ref.shape[0] - 1)]
        pltpu.make_async_copy(others, others, sem.at[at]).wait()

    for d in range(1, shards):
        send(stats_out, stats.at[s_me], 0, c_me, lax.rem(s_me + d, shards)).start()

    partial = dot(lifted[...], feat[...], ((0,), (0,)))
    mine = s_me * clips + c_me
    for at, flat, out, landing, first in (
        (1, sum_a, sum_out_a, sum_in_a, 0),
        (2, sum_b, sum_out_b, sum_in_b, send_cut),
    ):
        size = out.shape[1]
        for i in range(size):
            r, b = divmod(first + i, parts)
            flat[pl.ds(i, devices, stride=size), :] = partial[
                r * devices : (r + 1) * devices, b * LANES : (b + 1) * LANES
            ]
        out[...] = flat[...].reshape(out.shape).astype(BF16)
        for i in range(clips):
            for s in range(shards):
                c = lax.rem(c_me + i, clips)
                copy = send(out.at[c * shards + s], landing.at[mine], at, c, s)
                if i == 0:
                    pl.when(s_me != s)(copy.start)
                else:
                    copy.start()
    sum_in_a[mine] = sum_out_a[me]
    sum_in_b[mine] = sum_out_b[me]

    await_all(stats, 1)
    peaks = [stats[s, 0:1] for s in range(shards)]
    top = functools.reduce(jnp.maximum, peaks)
    lifts = [jnp.exp(p - top) for p in peaks]
    total = sum(stats[s, 1:2] * lifts[s] for s in range(shards))
    for s in range(shards):
        lift_out[s : s + 1] = lifts[s] / total
    lift[c_me] = lift_out[...]
    for d in range(1, clips):
        send(lift_out, lift.at[c_me], 3, lax.rem(c_me + d, clips), s_me).start()

    for i in range(CHUNKS):
        at = span(i)
        value = logits[at, :]
        weights = jnp.exp(value - jnp.max(value, axis=1, keepdims=True))
        combine[at, :] = (weights / jnp.sum(weights, axis=1, keepdims=True)).astype(BF16)

    await_all(lift, 7)
    lane = iota((clips, slots), 1)
    own = [
        [
            jnp.sum(
                jnp.where(lane == r * devices + me, lift[:, s, :], 0.0), axis=1, keepdims=True
            )
            for r in range(rows)
        ]
        for s in range(shards)
    ]

    def strip(low, high, cut, i, base, size):
        if i < cut:
            return low[pl.ds(base * cut + i, size, stride=cut), :]
        return high[pl.ds(base * (sub - cut) + i - cut, size, stride=sub - cut), :]

    def slot_rows(r):
        strips = []
        for b in range(parts):
            i = r * parts + b
            terms = [
                strip(sum_a, sum_b, send_cut, i, s * clips, clips) * own[s][r]
                for s in range(shards)
            ]
            strips.append(sum(terms[1:], terms[0]))
        return jnp.concatenate(strips, axis=1)

    def slot_inputs(e):
        wide = jnp.concatenate([slot_rows(e * each + q) for q in range(each)], axis=0)
        wide = wide.astype(BF16).astype(F32)
        mean = jnp.mean(wide * wide, axis=-1, keepdims=True)
        return (wide * lax.rsqrt(mean + 1e-06)).astype(BF16)

    steps = [slice(f, f + HIDDEN_CHUNK) for f in range(0, ff, HIDDEN_CHUNK)]

    def expand(e, normalized):
        hidden = []
        for at in steps:
            before = dot(normalized, w1_v[e, :, at]) + b1_v[:, at].astype(F32)[e : e + 1]
            value = 0.5 * before * (1.0 + lax.erf(before * math.sqrt(0.5)))
            hidden.append(value.astype(BF16))
        return hidden

    def reduce(e, hidden):
        out = b2_v[...].astype(F32)[e : e + 1]
        for at, value in zip(steps, hidden):
            out = out + dot(value, w2_v[e, at, :])
        out = out.astype(BF16).astype(F32)
        for q in range(each):
            for b in range(parts):
                i = (e * each + q) * parts + b
                back_packed[pl.ds(i, clips, stride=sub), :] = out[
                    q * clips : (q + 1) * clips, b * LANES : (b + 1) * LANES
                ]

    def back(at, c, s):
        out, landing = (back_out_a, back_in_a) if at == 4 else (back_out_b, back_in_b)
        return send(out.at[c], landing.at[me], at, c, s)

    def send_back(at, s):
        for c in range(clips):
            pl.when(me != c * shards + s)(back(at, c, s).start)

    for load in bias_loads:
        load.wait()
    for pair in weight_loads:
        for load in pair:
            load.wait()
    await_all(sum_in_a, 3)
    sum_a[...] = sum_in_a[...].astype(F32).reshape(sum_a.shape)
    first = expand(0, slot_inputs(0))
    await_all(sum_in_b, 5)
    sum_b[...] = sum_in_b[...].astype(F32).reshape(sum_b.shape)
    second = slot_inputs(1)
    reduce(0, first)
    second = expand(1, second)
    for c in range(clips):
        back_out_a[c] = back_packed[pl.ds(c * sub, back_cut), :].astype(BF16)
    send_back(4, 0)
    reduce(1, second)
    for c in range(clips):
        back_out_b[c] = back_packed[pl.ds(c * sub + back_cut, sub - back_cut), :].astype(BF16)
    send_back(5, 0)
    for s in range(1, shards):
        send_back(4, s)
        send_back(5, s)
    back_in_a[me] = back_out_a[c_me]
    back_in_b[me] = back_out_b[c_me]

    for at, landing, flat, first in (
        (9, back_in_a, back_a, 0),
        (11, back_in_b, back_b, back_cut),
    ):
        size = landing.shape[1]
        await_all(landing, at)
        flat[...] = landing[...].astype(F32).reshape(flat.shape)
        for i in range(size):
            r, b = divmod(first + i, parts)
            returned[r * devices : (r + 1) * devices, b * LANES : (b + 1) * LANES] = flat[
                pl.ds(i, devices, stride=size), :
            ].astype(BF16)
    for ref, at in (
        (stats, 0),
        (sum_in_a, 2),
        (sum_in_b, 4),
        (lift, 6),
        (back_in_a, 8),
        (back_in_b, 10),
    ):
        await_all(ref, at)


def mix(combine, returned, mixed, buffer, sems):
    stores = []
    for i in range(combine.shape[0] // MIX_CHUNK):
        at = pl.ds(i * MIX_CHUNK, MIX_CHUNK)
        buffer[at, :] = dot(combine[at, :], returned[...]).astype(BF16)
        store = pltpu.make_async_copy(buffer.at[at], mixed.at[at], sems.at[i])
        store.start()
        stores.append(store)
    for store in stores:
        store.wait()


def local(clips, shards, tokens, scales, slot_params, w1, b1, w2, b2):
    count, dim = tokens.shape[1:]
    blocks = scales.shape[1]
    slots = slot_params.shape[1]
    devices = clips * shards
    parts = dim // LANES
    sub = slots // devices * parts
    half = sub // w1.shape[0]
    send_cut = -(-half // TILE) * TILE
    back_cut = half // TILE * TILE

    def pieces(number, cut, dtype):
        if dtype == F32:
            return [pltpu.VMEM((number * n, LANES), F32) for n in (cut, sub - cut)]
        return [pltpu.VMEM((number, n, LANES), dtype) for n in (cut, sub - cut)]

    combine, returned = pl.pallas_call(
        functools.partial(kernel, clips, shards),
        out_shape=(pltpu.VMEM((count, slots), BF16), pltpu.VMEM((slots, dim), BF16)),
        in_specs=[pl.BlockSpec(memory_space=pltpu.HBM)] * 7,
        out_specs=(pl.BlockSpec(memory_space=pltpu.VMEM), pl.BlockSpec(memory_space=pltpu.VMEM)),
        scratch_shapes=[
            pltpu.VMEM((count, dim), BF16),
            pltpu.VMEM((blocks, 1, count), F32),
            pltpu.VMEM(slot_params.shape, BF16),
            pltpu.VMEM(w1.shape, BF16),
            pltpu.VMEM(b1.shape, BF16),
            pltpu.VMEM(w2.shape, BF16),
            pltpu.VMEM(b2.shape, BF16),
            pltpu.VMEM((count, slots), F32),
            pltpu.VMEM((count, slots), BF16),
            pltpu.VMEM((2, slots), F32),
            pltpu.VMEM((shards, 2, slots), F32),
            pltpu.VMEM((shards, slots), F32),
            pltpu.VMEM((clips, shards, slots), F32),
            *pieces(devices, send_cut, BF16),
            *pieces(devices, send_cut, BF16),
            *pieces(devices, send_cut, F32),
            pltpu.VMEM((clips * sub, LANES), F32),
            *pieces(clips, back_cut, BF16),
            *pieces(devices, back_cut, BF16),
            *pieces(devices, back_cut, F32),
            pltpu.SemaphoreType.DMA((4,)),
            pltpu.SemaphoreType.DMA((CHUNKS,)),
            pltpu.SemaphoreType.DMA((w1.shape[0], 2)),
            pltpu.SemaphoreType.DMA((12,)),
        ],
        compiler_params=pltpu.CompilerParams(
            collective_id=0, has_side_effects=True, vmem_limit_bytes=57 << 20
        ),
        name="slots",
    )(tokens[0], scales.transpose(1, 0, 2), slot_params, w1, b1, w2, b2)
    mixed = pl.pallas_call(
        mix,
        out_shape=jax.ShapeDtypeStruct((count, dim), BF16),
        in_specs=[pl.BlockSpec(memory_space=pltpu.VMEM)] * 2,
        out_specs=pl.BlockSpec(memory_space=pl.ANY),
        scratch_shapes=[
            pltpu.VMEM((count, dim), BF16),
            pltpu.SemaphoreType.DMA((count // MIX_CHUNK,)),
        ],
        compiler_params=pltpu.CompilerParams(vmem_limit_bytes=16 << 20),
        name="mix",
    )(combine, returned)
    return mixed[None]


def solution(mesh):
    placed = (
        P("clip", "shard", None),
        P("clip", None, "shard"),
        P(),
        P(("clip", "shard"), None, None),
        P(("clip", "shard"), None),
        P(("clip", "shard"), None, None),
        P(("clip", "shard"), None),
    )
    return jax.shard_map(
        functools.partial(local, mesh.shape["clip"], mesh.shape["shard"]),
        mesh=mesh,
        in_specs=placed,
        out_specs=P("clip", "shard", None),
        check_vma=False,
    )
```

```python
import functools
import math

import jax
import jax.numpy as jnp
from jax import lax
from jax.experimental import pallas as pl
from jax.experimental.pallas import tpu as pltpu
from jax.sharding import PartitionSpec as P

F32 = jnp.float32
BF16 = jnp.bfloat16
MESH = pl.DeviceIdType.MESH
CHUNKS = 2
MIX_CHUNK = 256
HIDDEN_CHUNK = 1536
LANES = 128
TILE = 8


def dot(a, b, contract=((1,), (0,))):
    return lax.dot_general(a, b, (contract, ((), ())), preferred_element_type=F32)


def iota(shape, axis):
    return lax.broadcasted_iota(jnp.int32, shape, axis)


def kernel(
    clips,
    shards,
    tokens,
    scales,
    slot_params,
    w1,
    b1,
    w2,
    b2,
    combine,
    returned,
    feat,
    scale_v,
    params_v,
    w1_v,
    b1_v,
    w2_v,
    b2_v,
    logits,
    lifted,
    stats_out,
    stats,
    lift_out,
    lift,
    sum_out_a,
    sum_out_b,
    sum_in_a,
    sum_in_b,
    sum_a,
    sum_b,
    back_packed,
    back_out_a,
    back_out_b,
    back_in_a,
    back_in_b,
    back_a,
    back_b,
    local_sem,
    token_sem,
    weight_sem,
    sem,
):
    c_me, s_me = lax.axis_index("clip"), lax.axis_index("shard")
    count, dim = feat.shape
    blocks = scale_v.shape[0]
    width = dim // blocks
    slots = params_v.shape[1]
    experts, _, ff = w1_v.shape
    devices = clips * shards
    rows = slots // devices
    each = rows // experts
    parts = dim // LANES
    sub = rows * parts
    send_cut = sum_in_a.shape[1]
    back_cut = back_in_a.shape[1]
    me = c_me * shards + s_me
    chunk = count // CHUNKS

    def span(i):
        return pl.ds(i * chunk, chunk)

    load_scale = pltpu.make_async_copy(scales, scale_v, local_sem.at[0])
    load_params = pltpu.make_async_copy(slot_params, params_v, local_sem.at[1])
    load_params.start()
    load_scale.start()
    for i in range(CHUNKS):
        pltpu.make_async_copy(tokens.at[span(i)], feat.at[span(i)], token_sem.at[i]).start()
    bias_loads = [
        pltpu.make_async_copy(b1, b1_v, local_sem.at[2]),
        pltpu.make_async_copy(b2, b2_v, local_sem.at[3]),
    ]
    weight_loads = [
        [
            pltpu.make_async_copy(w1.at[e], w1_v.at[e], weight_sem.at[e, 0]),
            pltpu.make_async_copy(w2.at[e], w2_v.at[e], weight_sem.at[e, 1]),
        ]
        for e in range(experts)
    ]
    barrier = pltpu.get_barrier_semaphore()

    def greet(d, carry):
        at = lax.rem(me + d, devices)
        to = (at // shards, lax.rem(at, shards))
        pl.semaphore_signal(barrier, inc=1, device_id=to, device_id_type=MESH)
        return carry

    lax.fori_loop(1, devices, greet, 0)
    load_params.wait()
    here, there = iota((slots, slots), 0), iota((slots, slots), 1)
    order = (here // rows == there % devices) & (here % rows == there // devices)
    params = dot(params_v[...], jnp.where(order, 1.0, 0.0).astype(BF16)).astype(BF16)
    load_scale.wait()

    def scale_rows(i):
        at = span(i)
        feat[at, :] = jnp.concatenate(
            [
                feat[at, b * width : (b + 1) * width].astype(F32)
                * jnp.broadcast_to(scale_v[b, 0:1, at], (width, chunk)).T
                for b in range(blocks)
            ],
            axis=1,
        ).astype(BF16)

    def score(i, peak):
        value = dot(feat[span(i), :], params)
        logits[span(i), :] = value
        return jnp.maximum(peak, jnp.max(value, axis=0, keepdims=True))

    peak = jnp.full((1, slots), -jnp.inf, F32)
    for i in range(CHUNKS):
        at = span(i)
        pltpu.make_async_copy(tokens.at[at], feat.at[at], token_sem.at[i]).wait()
        if i == CHUNKS - 1:
            for load in bias_loads:
                load.start()
            for pair in weight_loads:
                for load in pair:
                    load.start()
        if i > 0:
            peak = score(i - 1, peak)
        scale_rows(i)
    peak = score(CHUNKS - 1, peak)

    total = jnp.zeros((1, slots), F32)
    for i in range(CHUNKS):
        at = span(i)
        value = jnp.exp(logits[at, :] - peak)
        total = total + jnp.sum(value, axis=0, keepdims=True)
        lifted[at, :] = value.astype(BF16)
    stats_out[0:1, :] = peak
    stats_out[1:2, :] = total
    stats[s_me] = stats_out[...]
    pl.semaphore_wait(barrier, devices - 1)

    def send(src, dst, at, c, s):
        return pltpu.make_async_remote_copy(
            src_ref=src,
            dst_ref=dst,
            send_sem=sem.at[2 * at],
            recv_sem=sem.at[2 * at + 1],
            device_id=(c, s),
            device_id_type=MESH,
        )

    def await_all(ref, at):
        others = ref.at[pl.ds(0, ref.shape[0] - 1)]
        pltpu.make_async_copy(others, others, sem.at[at]).wait()

    for d in range(1, shards):
        send(stats_out, stats.at[s_me], 0, c_me, lax.rem(s_me + d, shards)).start()

    partial = dot(lifted[...], feat[...], ((0,), (0,)))
    mine = s_me * clips + c_me
    for at, flat, out, landing, first in (
        (1, sum_a, sum_out_a, sum_in_a, 0),
        (2, sum_b, sum_out_b, sum_in_b, send_cut),
    ):
        size = out.shape[1]
        for i in range(size):
            r, b = divmod(first + i, parts)
            flat[pl.ds(i, devices, stride=size), :] = partial[
                r * devices : (r + 1) * devices, b * LANES : (b + 1) * LANES
            ]
        out[...] = flat[...].reshape(out.shape).astype(BF16)
        for i in range(clips):
            for s in range(shards):
                c = lax.rem(c_me + i, clips)
                copy = send(out.at[c * shards + s], landing.at[mine], at, c, s)
                if i == 0:
                    pl.when(s_me != s)(copy.start)
                else:
                    copy.start()
    sum_in_a[mine] = sum_out_a[me]
    sum_in_b[mine] = sum_out_b[me]

    await_all(stats, 1)
    peaks = [stats[s, 0:1] for s in range(shards)]
    top = functools.reduce(jnp.maximum, peaks)
    lifts = [jnp.exp(p - top) for p in peaks]
    total = sum(stats[s, 1:2] * lifts[s] for s in range(shards))
    for s in range(shards):
        lift_out[s : s + 1] = lifts[s] / total
    lift[c_me] = lift_out[...]
    for d in range(1, clips):
        send(lift_out, lift.at[c_me], 3, lax.rem(c_me + d, clips), s_me).start()

    for i in range(CHUNKS):
        at = span(i)
        value = logits[at, :]
        weights = jnp.exp(value - jnp.max(value, axis=1, keepdims=True))
        combine[at, :] = (weights / jnp.sum(weights, axis=1, keepdims=True)).astype(BF16)

    await_all(lift, 7)
    lane = iota((clips, slots), 1)
    own = [
        [
            jnp.sum(
                jnp.where(lane == r * devices + me, lift[:, s, :], 0.0), axis=1, keepdims=True
            )
            for r in range(rows)
        ]
        for s in range(shards)
    ]

    def strip(low, high, cut, i, base, size):
        if i < cut:
            return low[pl.ds(base * cut + i, size, stride=cut), :]
        return high[pl.ds(base * (sub - cut) + i - cut, size, stride=sub - cut), :]

    def slot_rows(r):
        strips = []
        for b in range(parts):
            i = r * parts + b
            terms = [
                strip(sum_a, sum_b, send_cut, i, s * clips, clips) * own[s][r]
                for s in range(shards)
            ]
            strips.append(sum(terms[1:], terms[0]))
        return jnp.concatenate(strips, axis=1)

    def slot_inputs(e):
        wide = jnp.concatenate([slot_rows(e * each + q) for q in range(each)], axis=0)
        wide = wide.astype(BF16).astype(F32)
        mean = jnp.mean(wide * wide, axis=-1, keepdims=True)
        return (wide * lax.rsqrt(mean + 1e-06)).astype(BF16)

    steps = [slice(f, f + HIDDEN_CHUNK) for f in range(0, ff, HIDDEN_CHUNK)]

    def expand(e, normalized):
        hidden = []
        for at in steps:
            before = dot(normalized, w1_v[e, :, at]) + b1_v[:, at].astype(F32)[e : e + 1]
            value = 0.5 * before * (1.0 + lax.erf(before * math.sqrt(0.5)))
            hidden.append(value.astype(BF16))
        return hidden

    def reduce(e, hidden):
        out = b2_v[...].astype(F32)[e : e + 1]
        for at, value in zip(steps, hidden):
            out = out + dot(value, w2_v[e, at, :])
        out = out.astype(BF16).astype(F32)
        for q in range(each):
            for b in range(parts):
                i = (e * each + q) * parts + b
                back_packed[pl.ds(i, clips, stride=sub), :] = out[
                    q * clips : (q + 1) * clips, b * LANES : (b + 1) * LANES
                ]

    def back(at, c, s):
        out, landing = (back_out_a, back_in_a) if at == 4 else (back_out_b, back_in_b)
        return send(out.at[c], landing.at[me], at, c, s)

    def send_back(at, s):
        for c in range(clips):
            pl.when(me != c * shards + s)(back(at, c, s).start)

    for load in bias_loads:
        load.wait()
    for pair in weight_loads:
        for load in pair:
            load.wait()
    await_all(sum_in_a, 3)
    sum_a[...] = sum_in_a[...].astype(F32).reshape(sum_a.shape)
    first = expand(0, slot_inputs(0))
    await_all(sum_in_b, 5)
    sum_b[...] = sum_in_b[...].astype(F32).reshape(sum_b.shape)
    second = slot_inputs(1)
    reduce(0, first)
    second = expand(1, second)
    for c in range(clips):
        back_out_a[c] = back_packed[pl.ds(c * sub, back_cut), :].astype(BF16)
    for s in range(shards):
        send_back(4, s)
    reduce(1, second)
    for c in range(clips):
        back_out_b[c] = back_packed[pl.ds(c * sub + back_cut, sub - back_cut), :].astype(BF16)
    send_back(5, 0)
    for s in range(1, shards):
        send_back(5, s)
    back_in_a[me] = back_out_a[c_me]
    back_in_b[me] = back_out_b[c_me]

    for at, landing, flat, first in (
        (9, back_in_a, back_a, 0),
        (11, back_in_b, back_b, back_cut),
    ):
        size = landing.shape[1]
        await_all(landing, at)
        flat[...] = landing[...].astype(F32).reshape(flat.shape)
        for i in range(size):
            r, b = divmod(first + i, parts)
            returned[r * devices : (r + 1) * devices, b * LANES : (b + 1) * LANES] = flat[
                pl.ds(i, devices, stride=size), :
            ].astype(BF16)
    for ref, at in (
        (stats, 0),
        (sum_in_a, 2),
        (sum_in_b, 4),
        (lift, 6),
        (back_in_a, 8),
        (back_in_b, 10),
    ):
        await_all(ref, at)


def mix(combine, returned, mixed, buffer, sems):
    stores = []
    for i in range(combine.shape[0] // MIX_CHUNK):
        at = pl.ds(i * MIX_CHUNK, MIX_CHUNK)
        buffer[at, :] = dot(combine[at, :], returned[...]).astype(BF16)
        store = pltpu.make_async_copy(buffer.at[at], mixed.at[at], sems.at[i])
        store.start()
        stores.append(store)
    for store in stores:
        store.wait()


def local(clips, shards, tokens, scales, slot_params, w1, b1, w2, b2):
    count, dim = tokens.shape[1:]
    blocks = scales.shape[1]
    slots = slot_params.shape[1]
    devices = clips * shards
    parts = dim // LANES
    sub = slots // devices * parts
    half = sub // w1.shape[0]
    send_cut = -(-half // TILE) * TILE
    back_cut = half // TILE * TILE

    def pieces(number, cut, dtype):
        if dtype == F32:
            return [pltpu.VMEM((number * n, LANES), F32) for n in (cut, sub - cut)]
        return [pltpu.VMEM((number, n, LANES), dtype) for n in (cut, sub - cut)]

    combine, returned = pl.pallas_call(
        functools.partial(kernel, clips, shards),
        out_shape=(pltpu.VMEM((count, slots), BF16), pltpu.VMEM((slots, dim), BF16)),
        in_specs=[pl.BlockSpec(memory_space=pltpu.HBM)] * 7,
        out_specs=(pl.BlockSpec(memory_space=pltpu.VMEM), pl.BlockSpec(memory_space=pltpu.VMEM)),
        scratch_shapes=[
            pltpu.VMEM((count, dim), BF16),
            pltpu.VMEM((blocks, 1, count), F32),
            pltpu.VMEM(slot_params.shape, BF16),
            pltpu.VMEM(w1.shape, BF16),
            pltpu.VMEM(b1.shape, BF16),
            pltpu.VMEM(w2.shape, BF16),
            pltpu.VMEM(b2.shape, BF16),
            pltpu.VMEM((count, slots), F32),
            pltpu.VMEM((count, slots), BF16),
            pltpu.VMEM((2, slots), F32),
            pltpu.VMEM((shards, 2, slots), F32),
            pltpu.VMEM((shards, slots), F32),
            pltpu.VMEM((clips, shards, slots), F32),
            *pieces(devices, send_cut, BF16),
            *pieces(devices, send_cut, BF16),
            *pieces(devices, send_cut, F32),
            pltpu.VMEM((clips * sub, LANES), F32),
            *pieces(clips, back_cut, BF16),
            *pieces(devices, back_cut, BF16),
            *pieces(devices, back_cut, F32),
            pltpu.SemaphoreType.DMA((4,)),
            pltpu.SemaphoreType.DMA((CHUNKS,)),
            pltpu.SemaphoreType.DMA((w1.shape[0], 2)),
            pltpu.SemaphoreType.DMA((12,)),
        ],
        compiler_params=pltpu.CompilerParams(
            collective_id=0, has_side_effects=True, vmem_limit_bytes=57 << 20
        ),
        name="slots",
    )(tokens[0], scales.transpose(1, 0, 2), slot_params, w1, b1, w2, b2)
    mixed = pl.pallas_call(
        mix,
        out_shape=jax.ShapeDtypeStruct((count, dim), BF16),
        in_specs=[pl.BlockSpec(memory_space=pltpu.VMEM)] * 2,
        out_specs=pl.BlockSpec(memory_space=pl.ANY),
        scratch_shapes=[
            pltpu.VMEM((count, dim), BF16),
            pltpu.SemaphoreType.DMA((count // MIX_CHUNK,)),
        ],
        compiler_params=pltpu.CompilerParams(vmem_limit_bytes=16 << 20),
        name="mix",
    )(combine, returned)
    return mixed[None]


def solution(mesh):
    placed = (
        P("clip", "shard", None),
        P("clip", None, "shard"),
        P(),
        P(("clip", "shard"), None, None),
        P(("clip", "shard"), None),
        P(("clip", "shard"), None, None),
        P(("clip", "shard"), None),
    )
    return jax.shard_map(
        functools.partial(local, mesh.shape["clip"], mesh.shape["shard"]),
        mesh=mesh,
        in_specs=placed,
        out_specs=P("clip", "shard", None),
        check_vma=False,
    )
```
